512 devices in a mesh: seq: 64 (over x, z, core), head: 8 (over y).
Axes of the slice: x: 4, y: 8, z: 8, core: 2. Of those that a mesh axis runs over, the one named last changes fastest.
Arguments:
- queries: bfloat16 [32768, 4096], P(('seq', 'head'))
- key_vectors: bfloat16 [32768, 4096], P(('seq', 'head'))
- value_vectors: bfloat16 [32768, 4096], P(('seq', 'head')), may hold values from -6 to 6
- out_grads: bfloat16 [32768, 4096], P(('seq', 'head')), may hold values from -6 to 6
- extra_blocks: int32 [64, 8, 8], P('seq'), may hold values 0 or 1
- summary_rows: int32 [64, 16], P('seq'), may hold values from 0 to 511, as said below
Outputs:
- attention: bfloat16 [32768, 4096], P(('seq', 'head'))
- query_grad: bfloat16 [32768, 4096], P(('seq', 'head'))
- key_grad: bfloat16 [32768, 4096], P(('seq', 'head'))
- value_grad: bfloat16 [32768, 4096], P(('seq', 'head'))
The draws below stay inside these ranges and needn't reach their ends.
Inputs may be any that keep to these rules, and one draw needn't show every extreme that they name: `summary_rows`: summary row s of a group lies in [s * 32, (s + 1) * 32), so the rows of a group are distinct and ascending.
All inputs are finite; a program needn't handle non-finite values. No bound on the sum of `extra_blocks` on one device may be relied on, other than what follows from the above.
Results may differ from the reference program's by a relative error of at most 0.022.
Values may be sent and summed in bfloat16 or wider, within the bound.
A program may use at most 64 MiB of HBM per device.

```python
import jax
import jax.numpy as jnp
from jax import lax

HEADS = 32
HD = 128
GROUP = 512
SUMM = 16
NBLK = 8
GROUPS = 64
TOKENS = 32768
FEAT = 4096


def paired_fields(key):
    base = jax.random.fold_in(key, 4099)
    key_query, key_keys = jax.random.split(base, 2)
    row_count = TOKENS
    query_draw = 2.5 * jnp.clip(jax.random.normal(key_query, (row_count, HEADS, HD)), -6.0, 6.0)
    key_draw = jnp.clip(jax.random.normal(key_keys, (row_count, HEADS, HD)), -6.0, 6.0)
    return (query_draw.reshape(row_count, FEAT), key_draw.reshape(row_count, FEAT))


def draw_queries(key, part):
    return paired_fields(key)[0].astype(jnp.bfloat16)


def draw_key_vectors(key, part):
    return paired_fields(key)[1].astype(jnp.bfloat16)


def draw_summary_rows(key, part):
    stride = GROUP // SUMM
    offsets = jax.random.randint(jax.random.fold_in(key, 11), (GROUPS, SUMM), 0, stride)
    offsets = offsets.at[0, 0].set(0).at[0, SUMM - 1].set(stride - 1)
    return (jnp.arange(SUMM)[None, :] * stride + offsets).astype(jnp.int32)


def plant(values, stream_key, low, top_value):
    index_at = [jax.random.randint(jax.random.fold_in(stream_key, axis), (), 0, length) for axis, length in enumerate(values.shape)]
    main_axis = values.shape.index(max(values.shape))
    beside = index_at[:main_axis] + [(index_at[main_axis] + 1) % values.shape[main_axis]] + index_at[main_axis + 1:]
    return values.at[tuple(index_at)].set(low).at[tuple(beside)].set(top_value)


def levels(key, extent, pieces, smallest, high):
    def one(dim, shards_of):
        draws = jax.random.uniform(jax.random.fold_in(jax.random.fold_in(key, 6), dim), (shards_of,), jnp.float32, smallest / len(pieces), high / len(pieces))
        return jnp.repeat(jnp.exp(draws), extent[dim] // shards_of).reshape((-1,) + (1,) * (len(extent) - dim - 1))

    gain = one(*pieces[0])
    for cut in pieces[1:]:
        gain = gain * one(*cut)
    return gain


def bell_draw(rng, dims, deviation, bound, cuts=(), kind=jnp.bfloat16):
    entries = deviation * jax.random.normal(rng, dims, jnp.float32)
    if cuts:
        entries = entries * levels(rng, dims, cuts, -0.22, 0.18)
    return jnp.clip(entries, -bound, bound).astype(kind)


def setup_inputs(seed: int = 0) -> dict:
    seeds = jax.random.split(jax.random.key(seed), 7)
    return {
        "queries": draw_queries(jax.random.fold_in(seeds[6], 71), 0),
        "key_vectors": draw_key_vectors(jax.random.fold_in(seeds[6], 71), 0),
        "value_vectors": bell_draw(seeds[2], (TOKENS, FEAT), 1.0, 6.0, ((0, 512),)),
        "out_grads": bell_draw(seeds[3], (TOKENS, FEAT), 1.0, 6.0, ((0, 512),)),
        "extra_blocks": plant((jax.random.randint(seeds[4], (GROUPS, NBLK, NBLK), 0, 3) < 1).astype(jnp.int32), jax.random.fold_in(seeds[4], 1), 0, 1),
        "summary_rows": draw_summary_rows(jax.random.fold_in(seeds[6], 71), 0),
    }


neg_big = -1.0e30


def local_allowed(extra_map, group_len):
    block_count = extra_map.shape[0]
    block_len = group_len // block_count
    block_ids = jnp.arange(block_count, dtype=jnp.int32)
    block_lag = block_ids[:, None] - block_ids[None, :]
    allowed = (block_lag == 0) | (block_lag == 1) | ((extra_map == 1) & (block_lag > 0))
    allowed = jnp.repeat(jnp.repeat(allowed, block_len, axis=0), block_len, axis=1)
    positions = jnp.arange(group_len, dtype=jnp.int32)
    return allowed & (positions[None, :] <= positions[:, None])


def reference(queries, key_vectors, value_vectors, out_grads, extra_blocks, summary_rows):
    factor = HD ** -0.5
    query_heads = queries.reshape(GROUPS, GROUP, HEADS, HD)
    key_heads = key_vectors.reshape(GROUPS, GROUP, HEADS, HD)
    val_heads = value_vectors.reshape(GROUPS, GROUP, HEADS, HD)
    grad_heads = out_grads.reshape(GROUPS, GROUP, HEADS, HD)
    positions = (jnp.arange(GROUPS, dtype=jnp.int32)[:, None] * GROUP + summary_rows.astype(jnp.int32)).reshape(-1)
    summary_keys = key_vectors.reshape(TOKENS, HEADS, HD)[positions].astype(jnp.float32)
    summary_vals = value_vectors.reshape(TOKENS, HEADS, HD)[positions].astype(jnp.float32)
    owners = jnp.arange(GROUPS * SUMM, dtype=jnp.int32) // SUMM

    def advance(carried, inputs):
        key_sums, val_sums = carried
        query_c, key_c, val_c, grad_c, extra_map, rows_c, group_id = inputs
        allowed = jnp.concatenate([local_allowed(extra_map, GROUP), jnp.broadcast_to(owners[None, :] < group_id, (GROUP, GROUPS * SUMM))], axis=1)
        all_keys = jnp.concatenate([key_c.astype(jnp.float32), summary_keys], axis=0)
        all_vals = jnp.concatenate([val_c.astype(jnp.float32), summary_vals], axis=0)
        query_f = query_c.astype(jnp.float32)
        grad_f = grad_c.astype(jnp.float32)
        scores = jnp.where(allowed[None], jnp.einsum("qhd,khd->hqk", query_f, all_keys) * factor, neg_big)
        peak = jnp.max(scores, axis=2, keepdims=True)
        log_mass = jnp.log(jnp.sum(jnp.exp(scores - peak), axis=2, keepdims=True)) + peak
        attn_probs = jnp.where(allowed[None], jnp.exp(scores - log_mass), 0.0)
        weights = lax.optimization_barrier(attn_probs.astype(jnp.bfloat16)).astype(jnp.float32)
        attention = jnp.einsum("hqk,khd->qhd", weights, all_vals).astype(jnp.bfloat16)
        row_dot = jnp.einsum("qhd,qhd->hq", grad_f, attention.astype(jnp.float32))
        prob_grads = jnp.einsum("qhd,khd->hqk", grad_f, all_vals)
        score_grads = lax.optimization_barrier((attn_probs * (prob_grads - row_dot[..., None])).astype(jnp.bfloat16)).astype(jnp.float32)
        query_grad = (jnp.einsum("hqk,khd->qhd", score_grads, all_keys) * factor).astype(jnp.bfloat16)
        key_part = jnp.einsum("hqk,qhd->khd", score_grads, query_f) * factor
        val_part = jnp.einsum("hqk,qhd->khd", weights, grad_f)
        key_sums = key_sums + key_part[GROUP:]
        val_sums = val_sums + val_part[GROUP:]
        own_keys = lax.dynamic_slice_in_dim(key_sums, group_id * SUMM, SUMM, 0)
        own_vals = lax.dynamic_slice_in_dim(val_sums, group_id * SUMM, SUMM, 0)
        key_grad = key_part[:GROUP].at[rows_c].add(own_keys).astype(jnp.bfloat16)
        value_grad = val_part[:GROUP].at[rows_c].add(own_vals).astype(jnp.bfloat16)
        return (key_sums, val_sums), (attention, query_grad, key_grad, value_grad)

    start_sums = (jnp.zeros((GROUPS * SUMM, HEADS, HD), jnp.float32), jnp.zeros((GROUPS * SUMM, HEADS, HD), jnp.float32))
    inputs = (query_heads, key_heads, val_heads, grad_heads, extra_blocks, summary_rows.astype(jnp.int32), jnp.arange(GROUPS, dtype=jnp.int32))
    finals, stacked = lax.scan(advance, start_sums, inputs, reverse=True)
    attention, query_grad, key_grad, value_grad = stacked
    return (attention.reshape(TOKENS, FEAT), query_grad.reshape(TOKENS, FEAT), key_grad.reshape(TOKENS, FEAT), value_grad.reshape(TOKENS, FEAT))
```

```python
import functools
import math

import jax
import jax.numpy as jnp
from jax import lax
from jax.experimental import pallas as pl
from jax.experimental.pallas import tpu as pltpu
from jax.sharding import PartitionSpec as P

HD = 128
BF = jnp.bfloat16
F32 = jnp.float32
BIG = 3.0e38
NEG = -1.0e30


def split_seq(count):
    return {64: (4, 8, 2), 8: (2, 2, 2)}[count]


def dot_nn(a, b):
    return lax.dot_general(a, b, (((1,), (0,)), ((), ())), preferred_element_type=F32)


def dot_nt(a, b):
    return lax.dot_general(a, b, (((1,), (1,)), ((), ())), preferred_element_type=F32)


def dot_tn(a, b):
    return lax.dot_general(a, b, (((0,), (0,)), ((), ())), preferred_element_type=F32)


def spread(n):
    order = []
    for d in range(1, n // 2 + 1):
        order.append(d)
        if n - d != d:
            order.append(n - d)
    return order


def kernel(
    cfg,
    q_in, k_in, v_in, g_in, rows_ref, extra_ref,
    o_out, dq_out, dk_out, dv_out,
    kv, qg, skv, cap, sbuf, ebuf, stage, dloc, part, red1, red2, red3, psum,
    in_kv_send, in_qg_send, kv_recv, qg_recv,
    zg_send, zg_recv, xg_send, xg_recv, cg_send, cg_recv,
    cs_send, cs_recv, xs_send, xs_recv, zs_send, zs_recv,
    out_send, out_recv,
):
    nx, nz, nc, ny, heads, rows, summ, nblk = cfg
    group = rows * ny
    zrows = nz * summ
    tile = nc * zrows
    ins = (k_in, v_in, q_in, g_in)
    outs = (o_out, dq_out, dk_out, dv_out)
    factor = HD ** (-0.5)
    coef = factor * math.log2(math.e)

    seq = lax.axis_index("seq")
    y = lax.axis_index("head")
    x = seq // (nz * nc)
    z = (seq // nc) % nz
    c = seq % nc

    def at_y(yp):
        return (seq, yp)

    def at_z(zp):
        return (x * (nz * nc) + zp * nc + c, y)

    def at_x(xp):
        return (xp * (nz * nc) + z * nc + c, y)

    other = (x * (nz * nc) + z * nc + (1 - c), y)

    def remote(src, dst, send, recv, dev):
        return pltpu.make_async_remote_copy(
            src_ref=src, dst_ref=dst, send_sem=send, recv_sem=recv,
            device_id=dev, device_id_type=pl.DeviceIdType.MESH,
        )

    peers = [at_y(lax.rem(y + d, ny)) for d in range(1, ny)]
    peers += [at_z(lax.rem(z + d, nz)) for d in range(1, nz)]
    peers += [at_x(lax.rem(x + d, nx)) for d in range(1, nx)]
    peers += [other]
    barrier = pltpu.get_barrier_semaphore()
    for dev in peers:
        pl.semaphore_signal(barrier, inc=1, device_id=dev, device_id_type=pl.DeviceIdType.MESH)
    pl.semaphore_wait(barrier, len(peers))

    def cols(owner, h):
        return pl.ds(pl.multiple_of((owner * heads + h) * HD, HD), HD)

    def own_rows(owner):
        return pl.ds(pl.multiple_of(owner * rows, rows), rows)

    def send_inputs(h, buf, pair, send, recv):
        for a in range(2):
            pltpu.make_async_copy(
                ins[pair + a].at[:, cols(y, h)], buf.at[h, a, own_rows(y), :], recv.at[h]
            ).start()
        for d in spread(ny):
            yp = lax.rem(y + d, ny)
            for a in range(2):
                remote(
                    ins[pair + a].at[:, cols(yp, h)], buf.at[h, a, own_rows(y), :],
                    send, recv.at[h], at_y(yp),
                ).start()

    @pl.loop(0, heads)
    def _(h):
        send_inputs(h, kv, 0, in_kv_send, kv_recv)

    @pl.loop(0, heads)
    def _(h):
        send_inputs(h, qg, 2, in_qg_send, qg_recv)

    def drain(ref, sem):
        pltpu.make_async_copy(ref, ref, sem).wait()

    onehot = (
        lax.broadcasted_iota(jnp.int32, (summ, group), 1) == rows_ref[...]
    ).astype(F32).astype(BF)

    blen = group // nblk
    ids = lax.broadcasted_iota(jnp.int32, (nblk, group), 0)
    pos = lax.broadcasted_iota(jnp.int32, (nblk, group), 1)
    block_hot = (pos // blen == ids).astype(F32)
    chosen = (extra_ref[...] == 1).astype(F32)
    by_key = dot_nn(chosen, block_hot)
    reads = dot_tn(by_key, block_hot)
    key_pos = lax.broadcasted_iota(jnp.int32, (group, group), 0)
    query_pos = lax.broadcasted_iota(jnp.int32, (group, group), 1)
    lag = query_pos // blen - key_pos // blen
    allowed = (key_pos <= query_pos) & ((lag == 0) | (lag == 1) | ((lag > 0) & (reads > 0.5)))
    cap[...] = jnp.where(allowed, BIG, NEG)

    zslot = pl.ds(pl.multiple_of(z * summ, summ), summ)

    def gather_z(h):
        drain(kv.at[h], kv_recv.at[h])
        for a in range(2):
            skv[h, a, x, c, zslot, :] = dot_nn(onehot, kv[h, a]).astype(BF)
        for d in spread(nz):
            mine = skv.at[h, :, x, c, zslot, :]
            remote(mine, mine, zg_send, zg_recv.at[h], at_z(lax.rem(z + d, nz))).start()

    def gather_x(h):
        drain(skv.at[h, :, 0, 0, pl.ds(0, (nz - 1) * summ), :], zg_recv.at[h])
        for d in spread(nx):
            mine = skv.at[h, :, x, c]
            remote(mine, mine, xg_send, xg_recv.at[h], at_x(lax.rem(x + d, nx))).start()

    def gather_c(h):
        drain(skv.at[h, :, pl.ds(0, nx - 1), 0], xg_recv.at[h])
        mine = skv.at[h, :, :, c]
        remote(mine, mine, cg_send, cg_recv.at[h], other).start()

    @pl.loop(0, heads + 2)
    def _(t):
        @pl.when(t < heads)
        def _():
            gather_z(t)

        @pl.when((t >= 1) & (t < heads + 1))
        def _():
            gather_x(t - 1)

        @pl.when(t >= 2)
        def _():
            gather_c(t - 2)

    row_id = lax.broadcasted_iota(jnp.int32, (tile, 1), 0)
    row_order = ((row_id % zrows) // summ) * nc + row_id // zrows
    is_before = row_order < z * nc + c

    def send_outputs(h, arrays):
        for a in arrays:
            pltpu.make_async_copy(
                stage.at[h, a, own_rows(y), :], outs[a].at[:, cols(y, h)], out_recv.at[a]
            ).start()
        for d in spread(ny):
            yp = lax.rem(y + d, ny)
            for a in arrays:
                remote(
                    stage.at[h, a, own_rows(yp), :], outs[a].at[:, cols(y, h)],
                    out_send, out_recv.at[a], at_y(yp),
                ).start()

    def tile_rows(xp):
        return pl.ds(pl.multiple_of(group + xp * tile, tile), tile)

    def summary_tile(h, a, xp):
        return skv[h, a, xp].reshape(tile, HD)

    def attend(h):
        drain(qg.at[h], qg_recv.at[h])
        drain(skv.at[h, :, :, 0], cg_recv.at[h])
        q = qg[h, 0]
        scores = jnp.minimum(dot_nt(kv[h, 0], q), cap[...])
        sbuf[pl.ds(0, group), :] = scores
        peak = jnp.max(scores, axis=0, keepdims=True)

        def score_tile(xp, peak):
            scores = dot_nt(summary_tile(h, 0, xp), q)
            scores = jnp.minimum(scores, jnp.where((xp < x) | is_before, BIG, NEG))
            sbuf[tile_rows(xp), :] = scores
            return jnp.maximum(peak, jnp.max(scores, axis=0, keepdims=True))

        peak = lax.fori_loop(0, x + 1, score_tile, peak) * coef

        def exp_rows(place, vals, carried):
            mass, acc = carried
            e = jnp.exp2(sbuf[place, :] * coef - peak)
            eb = e.astype(BF)
            ebuf[place, :] = eb
            return mass + jnp.sum(e, axis=0, keepdims=True), acc + dot_tn(vals, eb)

        carried = (jnp.zeros((1, group), F32), jnp.zeros((HD, group), F32))
        carried = exp_rows(pl.ds(0, group), kv[h, 1], carried)
        mass, acc = lax.fori_loop(
            0, x + 1, lambda xp, cr: exp_rows(tile_rows(xp), summary_tile(h, 1, xp), cr), carried
        )
        inv = 1.0 / mass
        attn = (acc * inv).astype(BF).astype(F32)
        stage[h, 0] = attn.T.astype(BF)
        grad_t = qg[h, 1].astype(F32).T
        dot_row = jnp.sum(grad_t * attn, axis=0, keepdims=True) * inv
        grad_ts = grad_t * inv
        grad_tb = grad_ts.astype(BF)
        grad_b = grad_ts.T.astype(BF)

        def back_rows(place, keys, vals, acc):
            eb = ebuf[place, :]
            ds = (eb.astype(F32) * (dot_nn(vals, grad_tb) - dot_row)).astype(BF)
            return acc + dot_tn(keys, ds), dot_nn(ds, q) * factor, dot_nn(eb, grad_b)

        acc, dk, dv = back_rows(pl.ds(0, group), kv[h, 0], kv[h, 1], jnp.zeros((HD, group), F32))
        dloc[h, 0] = dk
        dloc[h, 1] = dv

        def back_tile(xp, acc):
            acc, dk, dv = back_rows(
                tile_rows(xp), summary_tile(h, 0, xp), summary_tile(h, 1, xp), acc
            )
            for cc in range(nc):
                part[h, xp, cc, 0] = dk[cc * zrows:(cc + 1) * zrows].astype(BF)
                part[h, xp, cc, 1] = dv[cc * zrows:(cc + 1) * zrows].astype(BF)
            return acc

        acc = lax.fori_loop(0, x + 1, back_tile, acc)
        stage[h, 1] = (acc * factor).T.astype(BF)
        send_outputs(h, (0, 1))

        @pl.loop(x + 1, nx)
        def _(xp):
            part[h, xp] = jnp.zeros(part.shape[2:], BF)

        mine = part.at[h, :, 1 - c]
        remote(mine, red1.at[h], cs_send, cs_recv.at[h], other).start()

    def reduce_c(h):
        drain(red1.at[h], cs_recv.at[h])

        @pl.loop(0, nx)
        def _(xp):
            part[h, xp, c] = (part[h, xp, c].astype(F32) + red1[h, xp].astype(F32)).astype(BF)

        for d in spread(nx):
            xp = lax.rem(x + d, nx)
            remote(part.at[h, xp, c], red2.at[h, x], xs_send, xs_recv.at[h], at_x(xp)).start()

    def reduce_x(h):
        drain(red2.at[h, pl.ds(0, nx - 1)], xs_recv.at[h])
        total = part[h, x, c].astype(F32)
        for d in range(1, nx):
            total += red2[h, lax.rem(x + d, nx)].astype(F32)
        psum[h] = total.astype(BF)
        for d in spread(nz):
            zp = lax.rem(z + d, nz)
            there = pl.ds(pl.multiple_of(zp * summ, summ), summ)
            remote(
                psum.at[h, :, there, :], red3.at[h, z], zs_send, zs_recv.at[h], at_z(zp)
            ).start()

    def reduce_z(h):
        drain(red3.at[h, pl.ds(0, nz - 1)], zs_recv.at[h])
        total = psum[h, :, zslot, :].astype(F32)
        for d in range(1, nz):
            total += red3[h, lax.rem(z + d, nz)].astype(F32)
        for a in range(2):
            high = total[a].astype(BF)
            low = (total[a] - high.astype(F32)).astype(BF)
            full = dloc[h, a] + dot_tn(onehot, high) + dot_tn(onehot, low)
            stage[h, 2 + a] = full.astype(BF)
        send_outputs(h, (2, 3))

    @pl.loop(0, heads + 3)
    def _(t):
        @pl.when(t < heads)
        def _():
            attend(t)

        @pl.when((t >= 1) & (t < heads + 1))
        def _():
            reduce_c(t - 1)

        @pl.when((t >= 2) & (t < heads + 2))
        def _():
            reduce_x(t - 2)

        @pl.when(t >= 3)
        def _():
            reduce_z(t - 3)

    for a in range(4):
        drain(outs[a], out_recv.at[a])
    sent = pl.ds(0, (ny - 1) * rows)
    drain(kv.at[:, :, sent, :], in_kv_send)
    drain(qg.at[:, :, sent, :], in_qg_send)
    drain(stage.at[:, :, sent, :], out_send)
    drain(skv.at[:, :, 0, 0, pl.ds(0, (nz - 1) * summ), :], zg_send)
    drain(skv.at[:, :, pl.ds(0, nx - 1), 0], xg_send)
    drain(skv.at[:, :, :, 0], cg_send)
    drain(red1, cs_send)
    drain(red2.at[:, pl.ds(0, nx - 1)], xs_send)
    drain(red3.at[:, pl.ds(0, nz - 1)], zs_send)


def per_device(queries, key_vectors, value_vectors, out_grads, extra_blocks, summary_rows):
    rows, feat = queries.shape
    ny = lax.axis_size("head")
    nx, nz, nc = split_seq(lax.axis_size("seq"))
    heads = feat // HD // ny
    summ = summary_rows.shape[1]
    nblk = extra_blocks.shape[1]
    group = rows * ny
    zrows = nz * summ
    keys = group + nx * nc * zrows
    cfg = (nx, nz, nc, ny, heads, rows, summ, nblk)
    dma = pltpu.SemaphoreType.DMA
    hbm = pl.BlockSpec(memory_space=pl.ANY)
    vmem = pl.BlockSpec(memory_space=pltpu.VMEM)
    return pl.pallas_call(
        functools.partial(kernel, cfg),
        out_shape=[jax.ShapeDtypeStruct((rows, feat), BF)] * 4,
        in_specs=[hbm] * 4 + [vmem] * 2,
        out_specs=[hbm] * 4,
        scratch_shapes=[
            pltpu.VMEM((heads, 2, group, HD), BF),
            pltpu.VMEM((heads, 2, group, HD), BF),
            pltpu.VMEM((heads, 2, nx, nc, zrows, HD), BF),
            pltpu.VMEM((group, group), F32),
            pltpu.VMEM((keys, group), F32),
            pltpu.VMEM((keys, group), BF),
            pltpu.VMEM((heads, 4, group, HD), BF),
            pltpu.VMEM((heads, 2, group, HD), F32),
            pltpu.VMEM((heads, nx, nc, 2, zrows, HD), BF),
            pltpu.VMEM((heads, nx, 2, zrows, HD), BF),
            pltpu.VMEM((heads, nx, 2, zrows, HD), BF),
            pltpu.VMEM((heads, nz, 2, summ, HD), BF),
            pltpu.VMEM((heads, 2, zrows, HD), BF),
            dma(()), dma(()), dma((heads,)), dma((heads,)),
            dma(()), dma((heads,)), dma(()), dma((heads,)), dma(()), dma((heads,)),
            dma(()), dma((heads,)), dma(()), dma((heads,)), dma(()), dma((heads,)),
            dma(()), dma((4,)),
        ],
        compiler_params=pltpu.CompilerParams(
            collective_id=0, has_side_effects=True, vmem_limit_bytes=48 * 1024 * 1024
        ),
    )(
        queries, key_vectors, value_vectors, out_grads,
        summary_rows.reshape(summ, 1), extra_blocks[0],
    )


def solution(mesh):
    tokens = P(("seq", "head"), None)
    return jax.shard_map(
        per_device,
        mesh=mesh,
        in_specs=(tokens,) * 4 + (P("seq", None, None), P("seq", None)),
        out_specs=(tokens,) * 4,
        check_vma=False,
    )
```

```python
import functools
import math

import jax
import jax.numpy as jnp
from jax import lax
from jax.experimental import pallas as pl
from jax.experimental.pallas import tpu as pltpu
from jax.sharding import PartitionSpec as P

HD = 128
BF = jnp.bfloat16
F32 = jnp.float32
BIG = 3.0e38
NEG = -1.0e30


def split_seq(count):
    return {64: (4, 8, 2), 8: (2, 2, 2)}[count]


def dot_nn(a, b):
    return lax.dot_general(a, b, (((1,), (0,)), ((), ())), preferred_element_type=F32)


def dot_nt(a, b):
    return lax.dot_general(a, b, (((1,), (1,)), ((), ())), preferred_element_type=F32)


def dot_tn(a, b):
    return lax.dot_general(a, b, (((0,), (0,)), ((), ())), preferred_element_type=F32)


def spread(n):
    order = []
    for d in range(1, n // 2 + 1):
        order.append(d)
        if n - d != d:
            order.append(n - d)
    return order


def kernel(
    cfg,
    q_in, k_in, v_in, g_in, rows_in, extra_in,
    o_out, dq_out, dk_out, dv_out,
    kv, qg, skv, cap, sbuf, ebuf, stage, dloc, part, red1, red2, red3, psum,
    in_kv_send, in_qg_send, kv_recv, qg_recv,
    zg_send, zg_recv, xg_send, xg_recv, cg_send, cg_recv,
    cs_send, cs_recv, xs_send, xs_recv, zs_send, zs_recv,
    out_send, out_recv, rows_ref, extra_ref, small_sem,
):
    nx, nz, nc, ny, heads, rows, summ, nblk = cfg
    group = rows * ny
    zrows = nz * summ
    tile = nc * zrows
    ins = (k_in, v_in, q_in, g_in)
    outs = (o_out, dq_out, dk_out, dv_out)
    factor = HD ** (-0.5)
    coef = factor * math.log2(math.e)

    seq = lax.axis_index("seq")
    y = lax.axis_index("head")
    x = seq // (nz * nc)
    z = (seq // nc) % nz
    c = seq % nc

    def at_y(yp):
        return (seq, yp)

    def at_z(zp):
        return (x * (nz * nc) + zp * nc + c, y)

    def at_x(xp):
        return (xp * (nz * nc) + z * nc + c, y)

    other = (x * (nz * nc) + z * nc + (1 - c), y)

    def remote(src, dst, send, recv, dev):
        return pltpu.make_async_remote_copy(
            src_ref=src, dst_ref=dst, send_sem=send, recv_sem=recv,
            device_id=dev, device_id_type=pl.DeviceIdType.MESH,
        )

    peers = [at_y(lax.rem(y + d, ny)) for d in range(1, ny)]
    peers += [at_z(lax.rem(z + d, nz)) for d in range(1, nz)]
    peers += [at_x(lax.rem(x + d, nx)) for d in range(1, nx)]
    peers += [other]
    barrier = pltpu.get_barrier_semaphore()
    for dev in peers:
        pl.semaphore_signal(barrier, inc=1, device_id=dev, device_id_type=pl.DeviceIdType.MESH)
    small = (
        pltpu.make_async_copy(rows_in, rows_ref, small_sem.at[0]),
        pltpu.make_async_copy(extra_in, extra_ref, small_sem.at[1]),
    )
    for copy in small:
        copy.start()
    pl.semaphore_wait(barrier, len(peers))

    def cols(owner, h):
        return pl.ds(pl.multiple_of((owner * heads + h) * HD, HD), HD)

    def own_rows(owner):
        return pl.ds(pl.multiple_of(owner * rows, rows), rows)

    def send_inputs(h, buf, pair, send, recv):
        for a in range(2):
            pltpu.make_async_copy(
                ins[pair + a].at[:, cols(y, h)], buf.at[h, a, own_rows(y), :], recv.at[h]
            ).start()
        for d in spread(ny):
            yp = lax.rem(y + d, ny)
            for a in range(2):
                remote(
                    ins[pair + a].at[:, cols(yp, h)], buf.at[h, a, own_rows(y), :],
                    send, recv.at[h], at_y(yp),
                ).start()

    @pl.loop(0, heads)
    def _(h):
        send_inputs(h, kv, 0, in_kv_send, kv_recv)

    @pl.loop(0, heads)
    def _(h):
        send_inputs(h, qg, 2, in_qg_send, qg_recv)

    def drain(ref, sem):
        pltpu.make_async_copy(ref, ref, sem).wait()

    for copy in small:
        copy.wait()
    onehot = (
        lax.broadcasted_iota(jnp.int32, (group, summ), 0) == rows_ref[...]
    ).astype(F32).astype(BF)

    blen = group // nblk
    ids = lax.broadcasted_iota(jnp.int32, (nblk, group), 0)
    pos = lax.broadcasted_iota(jnp.int32, (nblk, group), 1)
    block_hot = (pos // blen == ids).astype(F32)
    chosen = (extra_ref[0] == 1).astype(F32)
    by_key = dot_nn(chosen, block_hot)
    reads = dot_tn(by_key, block_hot)
    key_pos = lax.broadcasted_iota(jnp.int32, (group, group), 0)
    query_pos = lax.broadcasted_iota(jnp.int32, (group, group), 1)
    lag = query_pos // blen - key_pos // blen
    allowed = (key_pos <= query_pos) & ((lag == 0) | (lag == 1) | ((lag > 0) & (reads > 0.5)))
    cap[...] = jnp.where(allowed, BIG, NEG)

    zslot = pl.ds(pl.multiple_of(z * summ, summ), summ)

    def gather_z(h):
        drain(kv.at[h], kv_recv.at[h])
        for a in range(2):
            skv[h, a, x, c, zslot, :] = dot_tn(onehot, kv[h, a]).astype(BF)
        for d in spread(nz):
            mine = skv.at[h, :, x, c, zslot, :]
            remote(mine, mine, zg_send, zg_recv.at[h], at_z(lax.rem(z + d, nz))).start()

    def gather_x(h):
        drain(skv.at[h, :, 0, 0, pl.ds(0, (nz - 1) * summ), :], zg_recv.at[h])
        for d in spread(nx):
            mine = skv.at[h, :, x, c]
            remote(mine, mine, xg_send, xg_recv.at[h], at_x(lax.rem(x + d, nx))).start()

    def gather_c(h):
        drain(skv.at[h, :, pl.ds(0, nx - 1), 0], xg_recv.at[h])
        mine = skv.at[h, :, :, c]
        remote(mine, mine, cg_send, cg_recv.at[h], other).start()

    @pl.loop(0, heads + 2)
    def _(t):
        @pl.when(t < heads)
        def _():
            gather_z(t)

        @pl.when((t >= 1) & (t < heads + 1))
        def _():
            gather_x(t - 1)

        @pl.when(t >= 2)
        def _():
            gather_c(t - 2)

    row_id = lax.broadcasted_iota(jnp.int32, (tile, 1), 0)
    row_order = ((row_id % zrows) // summ) * nc + row_id // zrows
    is_before = row_order < z * nc + c

    def send_outputs(h, arrays):
        for a in arrays:
            pltpu.make_async_copy(
                stage.at[h, a, own_rows(y), :], outs[a].at[:, cols(y, h)], out_recv.at[a]
            ).start()
        for d in spread(ny):
            yp = lax.rem(y + d, ny)
            for a in arrays:
                remote(
                    stage.at[h, a, own_rows(yp), :], outs[a].at[:, cols(y, h)],
                    out_send, out_recv.at[a], at_y(yp),
                ).start()

    def tile_rows(xp):
        return pl.ds(pl.multiple_of(group + xp * tile, tile), tile)

    def summary_tile(h, a, xp):
        return skv[h, a, xp].reshape(tile, HD)

    def attend(h):
        drain(qg.at[h], qg_recv.at[h])
        drain(skv.at[h, :, :, 0], cg_recv.at[h])
        q = qg[h, 0]
        scores = jnp.minimum(dot_nt(kv[h, 0], q), cap[...])
        sbuf[pl.ds(0, group), :] = scores
        peak = jnp.max(scores, axis=0, keepdims=True)

        def score_tile(xp, peak):
            scores = dot_nt(summary_tile(h, 0, xp), q)
            scores = jnp.minimum(scores, jnp.where((xp < x) | is_before, BIG, NEG))
            sbuf[tile_rows(xp), :] = scores
            return jnp.maximum(peak, jnp.max(scores, axis=0, keepdims=True))

        peak = lax.fori_loop(0, x + 1, score_tile, peak) * coef

        def exp_rows(place, vals, carried):
            mass, acc = carried
            e = jnp.exp2(sbuf[place, :] * coef - peak)
            eb = e.astype(BF)
            ebuf[place, :] = eb
            return mass + jnp.sum(e, axis=0, keepdims=True), acc + dot_tn(vals, eb)

        carried = (jnp.zeros((1, group), F32), jnp.zeros((HD, group), F32))
        carried = exp_rows(pl.ds(0, group), kv[h, 1], carried)
        mass, acc = lax.fori_loop(
            0, x + 1, lambda xp, cr: exp_rows(tile_rows(xp), summary_tile(h, 1, xp), cr), carried
        )
        inv = 1.0 / mass
        attn = (acc * inv).astype(BF).astype(F32)
        stage[h, 0] = attn.T.astype(BF)
        grad_t = qg[h, 1].astype(F32).T
        dot_row = jnp.sum(grad_t * attn, axis=0, keepdims=True) * inv
        grad_ts = grad_t * inv
        grad_tb = grad_ts.astype(BF)
        grad_b = grad_ts.T.astype(BF)

        def back_rows(place, keys, vals, acc):
            eb = ebuf[place, :]
            ds = (eb.astype(F32) * (dot_nn(vals, grad_tb) - dot_row)).astype(BF)
            return acc + dot_tn(keys, ds), dot_nn(ds, q) * factor, dot_nn(eb, grad_b)

        acc, dk, dv = back_rows(pl.ds(0, group), kv[h, 0], kv[h, 1], jnp.zeros((HD, group), F32))
        dloc[h, 0] = dk
        dloc[h, 1] = dv

        def back_tile(xp, acc):
            acc, dk, dv = back_rows(
                tile_rows(xp), summary_tile(h, 0, xp), summary_tile(h, 1, xp), acc
            )
            for cc in range(nc):
                part[h, xp, cc, 0] = dk[cc * zrows:(cc + 1) * zrows].astype(BF)
                part[h, xp, cc, 1] = dv[cc * zrows:(cc + 1) * zrows].astype(BF)
            return acc

        acc = lax.fori_loop(0, x + 1, back_tile, acc)
        stage[h, 1] = (acc * factor).T.astype(BF)
        send_outputs(h, (0, 1))

        @pl.loop(x + 1, nx)
        def _(xp):
            part[h, xp] = jnp.zeros(part.shape[2:], BF)

        mine = part.at[h, :, 1 - c]
        remote(mine, red1.at[h], cs_send, cs_recv.at[h], other).start()

    def reduce_c(h):
        drain(red1.at[h], cs_recv.at[h])

        @pl.loop(0, nx)
        def _(xp):
            part[h, xp, c] = (part[h, xp, c].astype(F32) + red1[h, xp].astype(F32)).astype(BF)

        for d in spread(nx):
            xp = lax.rem(x + d, nx)
            remote(part.at[h, xp, c], red2.at[h, x], xs_send, xs_recv.at[h], at_x(xp)).start()

    def reduce_x(h):
        drain(red2.at[h, pl.ds(0, nx - 1)], xs_recv.at[h])
        total = part[h, x, c].astype(F32)
        for d in range(1, nx):
            total += red2[h, lax.rem(x + d, nx)].astype(F32)
        psum[h] = total.astype(BF)
        for d in spread(nz):
            zp = lax.rem(z + d, nz)
            there = pl.ds(pl.multiple_of(zp * summ, summ), summ)
            remote(
                psum.at[h, :, there, :], red3.at[h, z], zs_send, zs_recv.at[h], at_z(zp)
            ).start()

    def reduce_z(h):
        drain(red3.at[h, pl.ds(0, nz - 1)], zs_recv.at[h])
        total = psum[h, :, zslot, :].astype(F32)
        for d in range(1, nz):
            total += red3[h, lax.rem(z + d, nz)].astype(F32)
        for a in range(2):
            high = total[a].astype(BF)
            low = (total[a] - high.astype(F32)).astype(BF)
            full = dloc[h, a] + dot_nn(onehot, high) + dot_nn(onehot, low)
            stage[h, 2 + a] = full.astype(BF)
        send_outputs(h, (2, 3))

    @pl.loop(0, heads + 3)
    def _(t):
        @pl.when(t < heads)
        def _():
            attend(t)

        @pl.when((t >= 1) & (t < heads + 1))
        def _():
            reduce_c(t - 1)

        @pl.when((t >= 2) & (t < heads + 2))
        def _():
            reduce_x(t - 2)

        @pl.when(t >= 3)
        def _():
            reduce_z(t - 3)

    for a in range(4):
        drain(outs[a], out_recv.at[a])
    sent = pl.ds(0, (ny - 1) * rows)
    drain(kv.at[:, :, sent, :], in_kv_send)
    drain(qg.at[:, :, sent, :], in_qg_send)
    drain(stage.at[:, :, sent, :], out_send)
    drain(skv.at[:, :, 0, 0, pl.ds(0, (nz - 1) * summ), :], zg_send)
    drain(skv.at[:, :, pl.ds(0, nx - 1), 0], xg_send)
    drain(skv.at[:, :, :, 0], cg_send)
    drain(red1, cs_send)
    drain(red2.at[:, pl.ds(0, nx - 1)], xs_send)
    drain(red3.at[:, pl.ds(0, nz - 1)], zs_send)


def hand_over(a_in, b_in, c_in, d_in, a_out, b_out, c_out, d_out, buf, in_sems, out_sems):
    pieces = buf.shape[1]
    width = buf.shape[3]
    pairs = ((a_in, a_out), (b_in, b_out), (c_in, c_out), (d_in, d_out))
    loads, saves = [], []
    for i, (src, dst) in enumerate(pairs):
        for j in range(pieces):
            part = pl.ds(j * width, width)
            loads.append(pltpu.make_async_copy(src.at[:, part], buf.at[i, j], in_sems.at[i, j]))
            saves.append(pltpu.make_async_copy(buf.at[i, j], dst.at[:, part], out_sems.at[i, j]))
    for load in loads:
        load.start()
    for load, save in zip(loads, saves):
        load.wait()
        save.start()
    for save in saves:
        save.wait()


def per_device(queries, key_vectors, value_vectors, out_grads, extra_blocks, summary_rows):
    rows, feat = queries.shape
    ny = lax.axis_size("head")
    nx, nz, nc = split_seq(lax.axis_size("seq"))
    heads = feat // HD // ny
    summ = summary_rows.shape[1]
    nblk = extra_blocks.shape[1]
    group = rows * ny
    zrows = nz * summ
    keys = group + nx * nc * zrows
    cfg = (nx, nz, nc, ny, heads, rows, summ, nblk)
    dma = pltpu.SemaphoreType.DMA
    hbm = pl.BlockSpec(memory_space=pl.ANY)
    parts = pl.pallas_call(
        functools.partial(kernel, cfg),
        out_shape=[jax.ShapeDtypeStruct((rows, feat), BF)] * 4,
        in_specs=[hbm] * 6,
        out_specs=[hbm] * 4,
        scratch_shapes=[
            pltpu.VMEM((heads, 2, group, HD), BF),
            pltpu.VMEM((heads, 2, group, HD), BF),
            pltpu.VMEM((heads, 2, nx, nc, zrows, HD), BF),
            pltpu.VMEM((group, group), F32),
            pltpu.VMEM((keys, group), F32),
            pltpu.VMEM((keys, group), BF),
            pltpu.VMEM((heads, 4, group, HD), BF),
            pltpu.VMEM((heads, 2, group, HD), F32),
            pltpu.VMEM((heads, nx, nc, 2, zrows, HD), BF),
            pltpu.VMEM((heads, nx, 2, zrows, HD), BF),
            pltpu.VMEM((heads, nx, 2, zrows, HD), BF),
            pltpu.VMEM((heads, nz, 2, summ, HD), BF),
            pltpu.VMEM((heads, 2, zrows, HD), BF),
            dma(()), dma(()), dma((heads,)), dma((heads,)),
            dma(()), dma((heads,)), dma(()), dma((heads,)), dma(()), dma((heads,)),
            dma(()), dma((heads,)), dma(()), dma((heads,)), dma(()), dma((heads,)),
            dma(()), dma((4,)),
            pltpu.VMEM((1, summ), jnp.int32), pltpu.VMEM((1, nblk, nblk), jnp.int32), dma((2,)),
        ],
        compiler_params=pltpu.CompilerParams(
            collective_id=0, has_side_effects=True, vmem_limit_bytes=58 * 1024 * 1024
        ),
    )(
        queries, key_vectors, value_vectors, out_grads,
        summary_rows, extra_blocks,
    )
    return pl.pallas_call(
        hand_over,
        out_shape=[jax.ShapeDtypeStruct((rows, feat), BF)] * 4,
        in_specs=[hbm] * 4,
        out_specs=[hbm] * 4,
        scratch_shapes=[
            pltpu.VMEM((4, 2, rows, feat // 2), BF), dma((4, 2)), dma((4, 2)),
        ],
    )(*parts)


def solution(mesh):
    tokens = P(("seq", "head"), None)
    return jax.shard_map(
        per_device,
        mesh=mesh,
        in_specs=(tokens,) * 4 + (P("seq", None, None), P("seq", None)),
        out_specs=(tokens,) * 4,
        check_vma=False,
    )
```

```python
import functools
import math

import jax
import jax.numpy as jnp
from jax import lax
from jax.experimental import pallas as pl
from jax.experimental.pallas import tpu as pltpu
from jax.sharding import PartitionSpec as P

HD = 128
BF = jnp.bfloat16
F32 = jnp.float32
BIG = 3.0e38
NEG = -1.0e30


def split_seq(count):
    return {64: (4, 8, 2), 8: (2, 2, 2)}[count]


def dot_nn(a, b):
    return lax.dot_general(a, b, (((1,), (0,)), ((), ())), preferred_element_type=F32)


def dot_nt(a, b):
    return lax.dot_general(a, b, (((1,), (1,)), ((), ())), preferred_element_type=F32)


def dot_tn(a, b):
    return lax.dot_general(a, b, (((0,), (0,)), ((), ())), preferred_element_type=F32)


def spread(n):
    order = []
    for d in range(1, n // 2 + 1):
        order.append(d)
        if n - d != d:
            order.append(n - d)
    return order


def kernel(
    cfg,
    q_in, k_in, v_in, g_in, rows_in, extra_in,
    o_out, dq_out, dk_out, dv_out,
    kv, qg, skv, cap, sbuf, ebuf, stage, dloc, part, red1, red2, red3, psum,
    in_kv_send, in_qg_send, kv_recv, qg_recv,
    zg_send, zg_recv, xg_send, xg_recv, cg_send, cg_recv,
    cs_send, cs_recv, xs_send, xs_recv, zs_send, zs_recv,
    out_send, out_recv, rows_ref, extra_ref, small_sem, ring_ready, all_ready,
):
    nx, nz, nc, ny, heads, rows, summ, nblk = cfg
    group = rows * ny
    zrows = nz * summ
    tile = nc * zrows
    ins = (k_in, v_in, q_in, g_in)
    outs = (o_out, dq_out, dk_out, dv_out)
    factor = HD ** (-0.5)
    coef = factor * math.log2(math.e)

    seq = lax.axis_index("seq")
    y = lax.axis_index("head")
    x = seq // (nz * nc)
    z = (seq // nc) % nz
    c = seq % nc

    def at_y(yp):
        return (seq, yp)

    def at_z(zp):
        return (x * (nz * nc) + zp * nc + c, y)

    def at_x(xp):
        return (xp * (nz * nc) + z * nc + c, y)

    other = (x * (nz * nc) + z * nc + (1 - c), y)

    def remote(src, dst, send, recv, dev):
        return pltpu.make_async_remote_copy(
            src_ref=src, dst_ref=dst, send_sem=send, recv_sem=recv,
            device_id=dev, device_id_type=pl.DeviceIdType.MESH,
        )

    def signal(sem, dev):
        pl.semaphore_signal(sem, inc=1, device_id=dev, device_id_type=pl.DeviceIdType.MESH)

    barrier = pltpu.get_barrier_semaphore()
    for d in range(1, ny):
        yp = lax.rem(y + d, ny)

        @pl.when(yp != 0)
        def _():
            signal(barrier, at_y(yp))

    small = (
        pltpu.make_async_copy(rows_in, rows_ref, small_sem.at[0]),
        pltpu.make_async_copy(extra_in, extra_ref, small_sem.at[1]),
    )
    for copy in small:
        copy.start()

    @pl.when(y != 0)
    def _():
        pl.semaphore_wait(barrier, ny - 1)
        signal(ring_ready, at_y(0))

    rings = [at_z(lax.rem(z + d, nz)) for d in range(1, nz)]
    rings += [at_x(lax.rem(x + d, nx)) for d in range(1, nx)]
    rings += [other]

    @pl.when(y == 0)
    def _():
        pl.semaphore_wait(ring_ready, ny - 1)
        for dev in rings:
            signal(barrier, dev)

    def cols(owner, h):
        return pl.ds(pl.multiple_of((owner * heads + h) * HD, HD), HD)

    def own_rows(owner):
        return pl.ds(pl.multiple_of(owner * rows, rows), rows)

    def send_inputs(h, buf, pair, send, recv):
        for a in range(2):
            pltpu.make_async_copy(
                ins[pair + a].at[:, cols(y, h)], buf.at[h, a, own_rows(y), :], recv.at[h]
            ).start()
        for d in spread(ny):
            yp = lax.rem(y + d, ny)
            for a in range(2):
                remote(
                    ins[pair + a].at[:, cols(yp, h)], buf.at[h, a, own_rows(y), :],
                    send, recv.at[h], at_y(yp),
                ).start()

    @pl.loop(0, heads)
    def _(h):
        send_inputs(h, kv, 0, in_kv_send, kv_recv)

    @pl.loop(0, heads)
    def _(h):
        send_inputs(h, qg, 2, in_qg_send, qg_recv)

    def drain(ref, sem):
        pltpu.make_async_copy(ref, ref, sem).wait()

    for copy in small:
        copy.wait()
    onehot = (
        lax.broadcasted_iota(jnp.int32, (group, summ), 0) == rows_ref[...]
    ).astype(F32).astype(BF)

    blen = group // nblk
    ids = lax.broadcasted_iota(jnp.int32, (nblk, group), 0)
    pos = lax.broadcasted_iota(jnp.int32, (nblk, group), 1)
    block_hot = (pos // blen == ids).astype(F32)
    chosen = (extra_ref[0] == 1).astype(F32)
    by_key = dot_nn(chosen, block_hot)
    reads = dot_tn(by_key, block_hot)
    key_pos = lax.broadcasted_iota(jnp.int32, (group, group), 0)
    query_pos = lax.broadcasted_iota(jnp.int32, (group, group), 1)
    lag = query_pos // blen - key_pos // blen
    allowed = (key_pos <= query_pos) & ((lag == 0) | (lag == 1) | ((lag > 0) & (reads > 0.5)))
    cap[...] = jnp.where(allowed, BIG, NEG)

    zslot = pl.ds(pl.multiple_of(z * summ, summ), summ)

    def gather_z(h):
        drain(kv.at[h], kv_recv.at[h])
        for a in range(2):
            skv[h, a, x, c, zslot, :] = dot_tn(onehot, kv[h, a]).astype(BF)
        for d in spread(nz):
            mine = skv.at[h, :, x, c, zslot, :]
            remote(mine, mine, zg_send, zg_recv.at[h], at_z(lax.rem(z + d, nz))).start()

    def gather_x(h):
        drain(skv.at[h, :, 0, 0, pl.ds(0, (nz - 1) * summ), :], zg_recv.at[h])
        for d in spread(nx):
            mine = skv.at[h, :, x, c]
            remote(mine, mine, xg_send, xg_recv.at[h], at_x(lax.rem(x + d, nx))).start()

    def gather_c(h):
        drain(skv.at[h, :, pl.ds(0, nx - 1), 0], xg_recv.at[h])
        mine = skv.at[h, :, :, c]
        remote(mine, mine, cg_send, cg_recv.at[h], other).start()

    @pl.when(y == 0)
    def _():
        pl.semaphore_wait(barrier, len(rings))
        for d in range(1, ny):
            signal(all_ready, at_y(d))

    @pl.when(y != 0)
    def _():
        pl.semaphore_wait(all_ready, 1)

    @pl.loop(0, heads + 2)
    def _(t):
        @pl.when(t < heads)
        def _():
            gather_z(t)

        @pl.when((t >= 1) & (t < heads + 1))
        def _():
            gather_x(t - 1)

        @pl.when(t >= 2)
        def _():
            gather_c(t - 2)

    row_id = lax.broadcasted_iota(jnp.int32, (tile, 1), 0)
    row_order = ((row_id % zrows) // summ) * nc + row_id // zrows
    is_before = row_order < z * nc + c

    def send_outputs(h, arrays):
        for a in arrays:
            pltpu.make_async_copy(
                stage.at[h, a, own_rows(y), :], outs[a].at[:, cols(y, h)], out_recv.at[a]
            ).start()
        for d in spread(ny):
            yp = lax.rem(y + d, ny)
            for a in arrays:
                remote(
                    stage.at[h, a, own_rows(yp), :], outs[a].at[:, cols(y, h)],
                    out_send, out_recv.at[a], at_y(yp),
                ).start()

    def tile_rows(xp):
        return pl.ds(pl.multiple_of(group + xp * tile, tile), tile)

    def summary_tile(h, a, xp):
        return skv[h, a, xp].reshape(tile, HD)

    def attend(h):
        drain(qg.at[h], qg_recv.at[h])
        drain(skv.at[h, :, :, 0], cg_recv.at[h])
        q = qg[h, 0]
        scores = jnp.minimum(dot_nt(kv[h, 0], q), cap[...])
        sbuf[pl.ds(0, group), :] = scores
        peak = jnp.max(scores, axis=0, keepdims=True)

        def score_tile(xp, peak):
            scores = dot_nt(summary_tile(h, 0, xp), q)
            scores = jnp.minimum(scores, jnp.where((xp < x) | is_before, BIG, NEG))
            sbuf[tile_rows(xp), :] = scores
            return jnp.maximum(peak, jnp.max(scores, axis=0, keepdims=True))

        peak = lax.fori_loop(0, x + 1, score_tile, peak) * coef

        def exp_rows(place, vals, carried):
            mass, acc = carried
            e = jnp.exp2(sbuf[place, :] * coef - peak)
            eb = e.astype(BF)
            ebuf[place, :] = eb
            return mass + jnp.sum(e, axis=0, keepdims=True), acc + dot_tn(vals, eb)

        carried = (jnp.zeros((1, group), F32), jnp.zeros((HD, group), F32))
        carried = exp_rows(pl.ds(0, group), kv[h, 1], carried)
        mass, acc = lax.fori_loop(
            0, x + 1, lambda xp, cr: exp_rows(tile_rows(xp), summary_tile(h, 1, xp), cr), carried
        )
        inv = 1.0 / mass
        attn = (acc * inv).astype(BF).astype(F32)
        stage[h, 0] = attn.T.astype(BF)
        grad_t = qg[h, 1].astype(F32).T
        dot_row = jnp.sum(grad_t * attn, axis=0, keepdims=True) * inv
        grad_ts = grad_t * inv
        grad_tb = grad_ts.astype(BF)
        grad_b = grad_ts.T.astype(BF)

        def back_rows(place, keys, vals, acc):
            eb = ebuf[place, :]
            ds = (eb.astype(F32) * (dot_nn(vals, grad_tb) - dot_row)).astype(BF)
            return acc + dot_tn(keys, ds), dot_nn(ds, q) * factor, dot_nn(eb, grad_b)

        acc, dk, dv = back_rows(pl.ds(0, group), kv[h, 0], kv[h, 1], jnp.zeros((HD, group), F32))
        dloc[h, 0] = dk
        dloc[h, 1] = dv

        def back_tile(xp, acc):
            acc, dk, dv = back_rows(
                tile_rows(xp), summary_tile(h, 0, xp), summary_tile(h, 1, xp), acc
            )
            for cc in range(nc):
                part[h, xp, cc, 0] = dk[cc * zrows:(cc + 1) * zrows].astype(BF)
                part[h, xp, cc, 1] = dv[cc * zrows:(cc + 1) * zrows].astype(BF)
            return acc

        acc = lax.fori_loop(0, x + 1, back_tile, acc)
        stage[h, 1] = (acc * factor).T.astype(BF)
        send_outputs(h, (0, 1))

        @pl.loop(x + 1, nx)
        def _(xp):
            part[h, xp] = jnp.zeros(part.shape[2:], BF)

        mine = part.at[h, :, 1 - c]
        remote(mine, red1.at[h], cs_send, cs_recv.at[h], other).start()

    def reduce_c(h):
        drain(red1.at[h], cs_recv.at[h])

        @pl.loop(0, nx)
        def _(xp):
            part[h, xp, c] = (part[h, xp, c].astype(F32) + red1[h, xp].astype(F32)).astype(BF)

        for d in spread(nx):
            xp = lax.rem(x + d, nx)
            remote(part.at[h, xp, c], red2.at[h, x], xs_send, xs_recv.at[h], at_x(xp)).start()

    def reduce_x(h):
        drain(red2.at[h, pl.ds(0, nx - 1)], xs_recv.at[h])
        total = part[h, x, c].astype(F32)
        for d in range(1, nx):
            total += red2[h, lax.rem(x + d, nx)].astype(F32)
        psum[h] = total.astype(BF)
        for d in spread(nz):
            zp = lax.rem(z + d, nz)
            there = pl.ds(pl.multiple_of(zp * summ, summ), summ)
            remote(
                psum.at[h, :, there, :], red3.at[h, z], zs_send, zs_recv.at[h], at_z(zp)
            ).start()

    def reduce_z(h):
        drain(red3.at[h, pl.ds(0, nz - 1)], zs_recv.at[h])
        total = psum[h, :, zslot, :].astype(F32)
        for d in range(1, nz):
            total += red3[h, lax.rem(z + d, nz)].astype(F32)
        for a in range(2):
            high = total[a].astype(BF)
            low = (total[a] - high.astype(F32)).astype(BF)
            full = dloc[h, a] + dot_nn(onehot, high) + dot_nn(onehot, low)
            stage[h, 2 + a] = full.astype(BF)
        send_outputs(h, (2, 3))

    @pl.loop(0, heads + 3)
    def _(t):
        @pl.when(t < heads)
        def _():
            attend(t)

        @pl.when((t >= 1) & (t < heads + 1))
        def _():
            reduce_c(t - 1)

        @pl.when((t >= 2) & (t < heads + 2))
        def _():
            reduce_x(t - 2)

        @pl.when(t >= 3)
        def _():
            reduce_z(t - 3)

    for a in range(4):
        drain(outs[a], out_recv.at[a])
    sent = pl.ds(0, (ny - 1) * rows)
    drain(kv.at[:, :, sent, :], in_kv_send)
    drain(qg.at[:, :, sent, :], in_qg_send)
    drain(stage.at[:, :, sent, :], out_send)
    drain(skv.at[:, :, 0, 0, pl.ds(0, (nz - 1) * summ), :], zg_send)
    drain(skv.at[:, :, pl.ds(0, nx - 1), 0], xg_send)
    drain(skv.at[:, :, :, 0], cg_send)
    drain(red1, cs_send)
    drain(red2.at[:, pl.ds(0, nx - 1)], xs_send)
    drain(red3.at[:, pl.ds(0, nz - 1)], zs_send)


def hand_over(a_in, b_in, c_in, d_in, a_out, b_out, c_out, d_out, buf, in_sems, out_sems):
    pieces = buf.shape[1]
    width = buf.shape[3]
    pairs = ((a_in, a_out), (b_in, b_out), (c_in, c_out), (d_in, d_out))
    loads, saves = [], []
    for i, (src, dst) in enumerate(pairs):
        for j in range(pieces):
            part = pl.ds(j * width, width)
            loads.append(pltpu.make_async_copy(src.at[:, part], buf.at[i, j], in_sems.at[i, j]))
            saves.append(pltpu.make_async_copy(buf.at[i, j], dst.at[:, part], out_sems.at[i, j]))
    for load in loads:
        load.start()
    for load, save in zip(loads, saves):
        load.wait()
        save.start()
    for save in saves:
        save.wait()


def per_device(queries, key_vectors, value_vectors, out_grads, extra_blocks, summary_rows):
    rows, feat = queries.shape
    ny = lax.axis_size("head")
    nx, nz, nc = split_seq(lax.axis_size("seq"))
    heads = feat // HD // ny
    summ = summary_rows.shape[1]
    nblk = extra_blocks.shape[1]
    group = rows * ny
    zrows = nz * summ
    keys = group + nx * nc * zrows
    cfg = (nx, nz, nc, ny, heads, rows, summ, nblk)
    dma = pltpu.SemaphoreType.DMA
    hbm = pl.BlockSpec(memory_space=pl.ANY)
    parts = pl.pallas_call(
        functools.partial(kernel, cfg),
        out_shape=[jax.ShapeDtypeStruct((rows, feat), BF)] * 4,
        in_specs=[hbm] * 6,
        out_specs=[hbm] * 4,
        scratch_shapes=[
            pltpu.VMEM((heads, 2, group, HD), BF),
            pltpu.VMEM((heads, 2, group, HD), BF),
            pltpu.VMEM((heads, 2, nx, nc, zrows, HD), BF),
            pltpu.VMEM((group, group), F32),
            pltpu.VMEM((keys, group), F32),
            pltpu.VMEM((keys, group), BF),
            pltpu.VMEM((heads, 4, group, HD), BF),
            pltpu.VMEM((heads, 2, group, HD), F32),
            pltpu.VMEM((heads, nx, nc, 2, zrows, HD), BF),
            pltpu.VMEM((heads, nx, 2, zrows, HD), BF),
            pltpu.VMEM((heads, nx, 2, zrows, HD), BF),
            pltpu.VMEM((heads, nz, 2, summ, HD), BF),
            pltpu.VMEM((heads, 2, zrows, HD), BF),
            dma(()), dma(()), dma((heads,)), dma((heads,)),
            dma(()), dma((heads,)), dma(()), dma((heads,)), dma(()), dma((heads,)),
            dma(()), dma((heads,)), dma(()), dma((heads,)), dma(()), dma((heads,)),
            dma(()), dma((4,)),
            pltpu.VMEM((1, summ), jnp.int32), pltpu.VMEM((1, nblk, nblk), jnp.int32), dma((2,)),
            pltpu.SemaphoreType.REGULAR, pltpu.SemaphoreType.REGULAR,
        ],
        compiler_params=pltpu.CompilerParams(
            collective_id=0, has_side_effects=True, vmem_limit_bytes=58 * 1024 * 1024
        ),
    )(
        queries, key_vectors, value_vectors, out_grads,
        summary_rows, extra_blocks,
    )
    return pl.pallas_call(
        hand_over,
        out_shape=[jax.ShapeDtypeStruct((rows, feat), BF)] * 4,
        in_specs=[hbm] * 4,
        out_specs=[hbm] * 4,
        scratch_shapes=[
            pltpu.VMEM((4, 2, rows, feat // 2), BF), dma((4, 2)), dma((4, 2)),
        ],
    )(*parts)


def solution(mesh):
    tokens = P(("seq", "head"), None)
    return jax.shard_map(
        per_device,
        mesh=mesh,
        in_specs=(tokens,) * 4 + (P("seq", None, None), P("seq", None)),
        out_specs=(tokens,) * 4,
        check_vma=False,
    )
```

```python
import functools
import math

import jax
import jax.numpy as jnp
from jax import lax
from jax.experimental import pallas as pl
from jax.experimental.pallas import tpu as pltpu
from jax.sharding import PartitionSpec as P

HD = 128
BF = jnp.bfloat16
F32 = jnp.float32
BIG = 3.0e38
NEG = -1.0e30


def split_seq(count):
    return {64: (4, 8, 2), 8: (2, 2, 2)}[count]


def dot_nn(a, b):
    return lax.dot_general(a, b, (((1,), (0,)), ((), ())), preferred_element_type=F32)


def dot_nt(a, b):
    return lax.dot_general(a, b, (((1,), (1,)), ((), ())), preferred_element_type=F32)


def dot_tn(a, b):
    return lax.dot_general(a, b, (((0,), (0,)), ((), ())), preferred_element_type=F32)


def spread(n):
    order = []
    for d in range(1, n // 2 + 1):
        order.append(d)
        if n - d != d:
            order.append(n - d)
    return order


def kernel(
    cfg,
    q_in, k_in, v_in, g_in, rows_in, extra_in,
    o_out, dq_out, dk_out, dv_out,
    kv, qg, skv, cap, sbuf, ebuf, stage, dloc, part, red1, red2, red3, psum,
    in_kv_send, in_qg_send, kv_recv, qg_recv,
    zg_send, zg_recv, xg_send, xg_recv, cg_send, cg_recv,
    cs_send, cs_recv, xs_send, xs_recv, zs_send, zs_recv,
    out_send, out_recv, rows_ref, extra_ref, small_sem, ring_ready, all_ready,
):
    nx, nz, nc, ny, heads, rows, summ, nblk = cfg
    group = rows * ny
    zrows = nz * summ
    tile = nc * zrows
    ins = (k_in, v_in, q_in, g_in)
    outs = (o_out, dq_out, dk_out, dv_out)
    factor = HD ** (-0.5)
    coef = factor * math.log2(math.e)

    seq = lax.axis_index("seq")
    y = lax.axis_index("head")
    x = seq // (nz * nc)
    z = (seq // nc) % nz
    c = seq % nc

    def at_y(yp):
        return (seq, yp)

    def at_z(zp):
        return (x * (nz * nc) + zp * nc + c, y)

    def at_x(xp):
        return (xp * (nz * nc) + z * nc + c, y)

    other = (x * (nz * nc) + z * nc + (1 - c), y)

    def remote(src, dst, send, recv, dev):
        return pltpu.make_async_remote_copy(
            src_ref=src, dst_ref=dst, send_sem=send, recv_sem=recv,
            device_id=dev, device_id_type=pl.DeviceIdType.MESH,
        )

    def signal(sem, dev):
        pl.semaphore_signal(sem, inc=1, device_id=dev, device_id_type=pl.DeviceIdType.MESH)

    barrier = pltpu.get_barrier_semaphore()
    for d in range(1, ny):
        yp = lax.rem(y + d, ny)

        @pl.when(yp != 0)
        def _():
            signal(barrier, at_y(yp))

    small = (
        pltpu.make_async_copy(rows_in, rows_ref, small_sem.at[0]),
        pltpu.make_async_copy(extra_in, extra_ref, small_sem.at[1]),
    )
    for copy in small:
        copy.start()

    @pl.when(y != 0)
    def _():
        pl.semaphore_wait(barrier, ny - 1)
        signal(ring_ready, at_y(0))

    rings = [at_z(lax.rem(z + d, nz)) for d in range(1, nz)]
    rings += [at_x(lax.rem(x + d, nx)) for d in range(1, nx)]
    rings += [other]

    @pl.when(y == 0)
    def _():
        pl.semaphore_wait(ring_ready, ny - 1)
        for dev in rings:
            signal(barrier, dev)

    def cols(owner, h):
        return pl.ds(pl.multiple_of((owner * heads + h) * HD, HD), HD)

    def own_rows(owner):
        return pl.ds(pl.multiple_of(owner * rows, rows), rows)

    def send_inputs(h, buf, pair, send, recv):
        for a in range(2):
            pltpu.make_async_copy(
                ins[pair + a].at[:, cols(y, h)], buf.at[h, a, own_rows(y), :], recv.at[h]
            ).start()
        for d in spread(ny):
            yp = lax.rem(y + d, ny)
            for a in range(2):
                remote(
                    ins[pair + a].at[:, cols(yp, h)], buf.at[h, a, own_rows(y), :],
                    send, recv.at[h], at_y(yp),
                ).start()

    @pl.loop(0, heads)
    def _(h):
        send_inputs(h, kv, 0, in_kv_send, kv_recv)

    @pl.loop(0, heads)
    def _(h):
        send_inputs(h, qg, 2, in_qg_send, qg_recv)

    def drain(ref, sem):
        pltpu.make_async_copy(ref, ref, sem).wait()

    for copy in small:
        copy.wait()
    onehot = (
        lax.broadcasted_iota(jnp.int32, (group, summ), 0) == rows_ref[...]
    ).astype(F32).astype(BF)

    blen = group // nblk
    ids = lax.broadcasted_iota(jnp.int32, (nblk, group), 0)
    pos = lax.broadcasted_iota(jnp.int32, (nblk, group), 1)
    block_hot = (pos // blen == ids).astype(F32)
    chosen = (extra_ref[0] == 1).astype(F32)
    by_key = dot_nn(chosen, block_hot)
    reads = dot_tn(by_key, block_hot)
    key_pos = lax.broadcasted_iota(jnp.int32, (group, group), 0)
    query_pos = lax.broadcasted_iota(jnp.int32, (group, group), 1)
    lag = query_pos // blen - key_pos // blen
    allowed = (key_pos <= query_pos) & ((lag == 0) | (lag == 1) | ((lag > 0) & (reads > 0.5)))
    cap[...] = jnp.where(allowed, BIG, NEG)

    zslot = pl.ds(pl.multiple_of(z * summ, summ), summ)

    def gather_z(h):
        drain(kv.at[h], kv_recv.at[h])
        for a in range(2):
            skv[h, a, x, c, zslot, :] = dot_tn(onehot, kv[h, a]).astype(BF)
        for d in spread(nz):
            mine = skv.at[h, :, x, c, zslot, :]
            remote(mine, mine, zg_send, zg_recv.at[h], at_z(lax.rem(z + d, nz))).start()

    def gather_x(h):
        drain(skv.at[h, :, 0, 0, pl.ds(0, (nz - 1) * summ), :], zg_recv.at[h])
        for d in spread(nx):
            mine = skv.at[h, :, x, c]
            remote(mine, mine, xg_send, xg_recv.at[h], at_x(lax.rem(x + d, nx))).start()

    def gather_c(h):
        drain(skv.at[h, :, pl.ds(0, nx - 1), 0], xg_recv.at[h])
        mine = skv.at[h, :, :, c]
        remote(mine, mine, cg_send, cg_recv.at[h], other).start()

    @pl.when(y == 0)
    def _():
        pl.semaphore_wait(barrier, len(rings))
        for d in range(1, ny):
            signal(all_ready, at_y(d))

    @pl.when(y != 0)
    def _():
        pl.semaphore_wait(all_ready, 1)

    @pl.loop(0, heads + 2)
    def _(t):
        @pl.when(t < heads)
        def _():
            gather_z(t)

        @pl.when((t >= 1) & (t < heads + 1))
        def _():
            gather_x(t - 1)

        @pl.when(t >= 2)
        def _():
            gather_c(t - 2)

    row_id = lax.broadcasted_iota(jnp.int32, (tile, 1), 0)
    row_order = ((row_id % zrows) // summ) * nc + row_id // zrows
    is_before = row_order < z * nc + c

    def send_outputs(h, arrays):
        for a in arrays:
            pltpu.make_async_copy(
                stage.at[h, a, own_rows(y), :], outs[a].at[:, cols(y, h)], out_recv.at[a]
            ).start()
        for d in spread(ny):
            yp = lax.rem(y + d, ny)
            for a in arrays:
                remote(
                    stage.at[h, a, own_rows(yp), :], outs[a].at[:, cols(y, h)],
                    out_send, out_recv.at[a], at_y(yp),
                ).start()

    def attend(h, tiles):
        q = qg[h, 0]
        spans = [(pl.ds(0, group), kv[h, 0], kv[h, 1])]
        for xp in range(tiles):
            spans.append((
                pl.ds(group + xp * tile, tile),
                skv[h, 0, xp].reshape(tile, HD),
                skv[h, 1, xp].reshape(tile, HD),
            ))
        peak = None
        for i, (place, keys, _) in enumerate(spans):
            scores = dot_nt(keys, q)
            if i == 0:
                scores = jnp.minimum(scores, cap[...])
            elif i == tiles:
                scores = jnp.minimum(scores, jnp.where(is_before, BIG, NEG))
            sbuf[place, :] = scores
            top = jnp.max(scores, axis=0, keepdims=True)
            peak = top if peak is None else jnp.maximum(peak, top)
        peak = peak * coef
        mass = jnp.zeros((1, group), F32)
        acc = jnp.zeros((HD, group), F32)
        for place, _, vals in spans:
            e = jnp.exp2(sbuf[place, :] * coef - peak)
            eb = e.astype(BF)
            ebuf[place, :] = eb
            mass += jnp.sum(e, axis=0, keepdims=True)
            acc += dot_tn(vals, eb)
        inv = 1.0 / mass
        attn = (acc * inv).astype(BF).astype(F32)
        stage[h, 0] = attn.T.astype(BF)
        grad_t = qg[h, 1].astype(F32).T
        dot_row = jnp.sum(grad_t * attn, axis=0, keepdims=True) * inv
        grad_ts = grad_t * inv
        grad_tb = grad_ts.astype(BF)
        grad_b = grad_ts.T.astype(BF)
        acc = jnp.zeros((HD, group), F32)
        for i, (place, keys, vals) in enumerate(spans):
            eb = ebuf[place, :]
            ds = (eb.astype(F32) * (dot_nn(vals, grad_tb) - dot_row)).astype(BF)
            acc += dot_tn(keys, ds)
            dk = dot_nn(ds, q) * factor
            dv = dot_nn(eb, grad_b)
            if i == 0:
                dloc[h, 0] = dk
                dloc[h, 1] = dv
            else:
                for cc in range(nc):
                    rows_c = slice(cc * zrows, (cc + 1) * zrows)
                    part[h, i - 1, cc, 0] = dk[rows_c].astype(BF)
                    part[h, i - 1, cc, 1] = dv[rows_c].astype(BF)
        stage[h, 1] = (acc * factor).T.astype(BF)
        for xp in range(tiles, nx):
            part[h, xp] = jnp.zeros(part.shape[2:], BF)

    def attend_send(h):
        drain(qg.at[h], qg_recv.at[h])
        drain(skv.at[h, :, :, 0], cg_recv.at[h])
        for tiles in range(1, nx + 1):

            @pl.when(x == tiles - 1)
            def _():
                attend(h, tiles)

        send_outputs(h, (0, 1))

        mine = part.at[h, :, 1 - c]
        remote(mine, red1.at[h], cs_send, cs_recv.at[h], other).start()

    def reduce_c(h):
        drain(red1.at[h], cs_recv.at[h])

        @pl.loop(0, nx)
        def _(xp):
            part[h, xp, c] = (part[h, xp, c].astype(F32) + red1[h, xp].astype(F32)).astype(BF)

        for d in spread(nx):
            xp = lax.rem(x + d, nx)
            remote(part.at[h, xp, c], red2.at[h, x], xs_send, xs_recv.at[h], at_x(xp)).start()

    def reduce_x(h):
        drain(red2.at[h, pl.ds(0, nx - 1)], xs_recv.at[h])
        total = part[h, x, c].astype(F32)
        for d in range(1, nx):
            total += red2[h, lax.rem(x + d, nx)].astype(F32)
        psum[h] = total.astype(BF)
        for d in spread(nz):
            zp = lax.rem(z + d, nz)
            there = pl.ds(pl.multiple_of(zp * summ, summ), summ)
            remote(
                psum.at[h, :, there, :], red3.at[h, z], zs_send, zs_recv.at[h], at_z(zp)
            ).start()

    def reduce_z(h):
        drain(red3.at[h, pl.ds(0, nz - 1)], zs_recv.at[h])
        total = psum[h, :, zslot, :].astype(F32)
        for d in range(1, nz):
            total += red3[h, lax.rem(z + d, nz)].astype(F32)
        for a in range(2):
            high = total[a].astype(BF)
            low = (total[a] - high.astype(F32)).astype(BF)
            full = dloc[h, a] + dot_nn(onehot, high) + dot_nn(onehot, low)
            stage[h, 2 + a] = full.astype(BF)
        send_outputs(h, (2, 3))

    @pl.loop(0, heads + 3)
    def _(t):
        @pl.when(t < heads)
        def _():
            attend_send(t)

        @pl.when((t >= 1) & (t < heads + 1))
        def _():
            reduce_c(t - 1)

        @pl.when((t >= 2) & (t < heads + 2))
        def _():
            reduce_x(t - 2)

        @pl.when(t >= 3)
        def _():
            reduce_z(t - 3)

    for a in range(4):
        drain(outs[a], out_recv.at[a])
    sent = pl.ds(0, (ny - 1) * rows)
    drain(kv.at[:, :, sent, :], in_kv_send)
    drain(qg.at[:, :, sent, :], in_qg_send)
    drain(stage.at[:, :, sent, :], out_send)
    drain(skv.at[:, :, 0, 0, pl.ds(0, (nz - 1) * summ), :], zg_send)
    drain(skv.at[:, :, pl.ds(0, nx - 1), 0], xg_send)
    drain(skv.at[:, :, :, 0], cg_send)
    drain(red1, cs_send)
    drain(red2.at[:, pl.ds(0, nx - 1)], xs_send)
    drain(red3.at[:, pl.ds(0, nz - 1)], zs_send)


def hand_over(a_in, b_in, c_in, d_in, a_out, b_out, c_out, d_out, buf, in_sems, out_sems):
    pieces = buf.shape[1]
    width = buf.shape[3]
    pairs = ((a_in, a_out), (b_in, b_out), (c_in, c_out), (d_in, d_out))
    loads, saves = [], []
    for i, (src, dst) in enumerate(pairs):
        for j in range(pieces):
            part = pl.ds(j * width, width)
            loads.append(pltpu.make_async_copy(src.at[:, part], buf.at[i, j], in_sems.at[i, j]))
            saves.append(pltpu.make_async_copy(buf.at[i, j], dst.at[:, part], out_sems.at[i, j]))
    for load in loads:
        load.start()
    for load, save in zip(loads, saves):
        load.wait()
        save.start()
    for save in saves:
        save.wait()


def per_device(queries, key_vectors, value_vectors, out_grads, extra_blocks, summary_rows):
    rows, feat = queries.shape
    ny = lax.axis_size("head")
    nx, nz, nc = split_seq(lax.axis_size("seq"))
    heads = feat // HD // ny
    summ = summary_rows.shape[1]
    nblk = extra_blocks.shape[1]
    group = rows * ny
    zrows = nz * summ
    keys = group + nx * nc * zrows
    cfg = (nx, nz, nc, ny, heads, rows, summ, nblk)
    dma = pltpu.SemaphoreType.DMA
    hbm = pl.BlockSpec(memory_space=pl.ANY)
    parts = pl.pallas_call(
        functools.partial(kernel, cfg),
        out_shape=[jax.ShapeDtypeStruct((rows, feat), BF)] * 4,
        in_specs=[hbm] * 6,
        out_specs=[hbm] * 4,
        scratch_shapes=[
            pltpu.VMEM((heads, 2, group, HD), BF),
            pltpu.VMEM((heads, 2, group, HD), BF),
            pltpu.VMEM((heads, 2, nx, nc, zrows, HD), BF),
            pltpu.VMEM((group, group), F32),
            pltpu.VMEM((keys, group), F32),
            pltpu.VMEM((keys, group), BF),
            pltpu.VMEM((heads, 4, group, HD), BF),
            pltpu.VMEM((heads, 2, group, HD), F32),
            pltpu.VMEM((heads, nx, nc, 2, zrows, HD), BF),
            pltpu.VMEM((heads, nx, 2, zrows, HD), BF),
            pltpu.VMEM((heads, nx, 2, zrows, HD), BF),
            pltpu.VMEM((heads, nz, 2, summ, HD), BF),
            pltpu.VMEM((heads, 2, zrows, HD), BF),
            dma(()), dma(()), dma((heads,)), dma((heads,)),
            dma(()), dma((heads,)), dma(()), dma((heads,)), dma(()), dma((heads,)),
            dma(()), dma((heads,)), dma(()), dma((heads,)), dma(()), dma((heads,)),
            dma(()), dma((4,)),
            pltpu.VMEM((1, summ), jnp.int32), pltpu.VMEM((1, nblk, nblk), jnp.int32), dma((2,)),
            pltpu.SemaphoreType.REGULAR, pltpu.SemaphoreType.REGULAR,
        ],
        compiler_params=pltpu.CompilerParams(
            collective_id=0, has_side_effects=True, vmem_limit_bytes=58 * 1024 * 1024
        ),
    )(
        queries, key_vectors, value_vectors, out_grads,
        summary_rows, extra_blocks,
    )
    return pl.pallas_call(
        hand_over,
        out_shape=[jax.ShapeDtypeStruct((rows, feat), BF)] * 4,
        in_specs=[hbm] * 4,
        out_specs=[hbm] * 4,
        scratch_shapes=[
            pltpu.VMEM((4, 2, rows, feat // 2), BF), dma((4, 2)), dma((4, 2)),
        ],
    )(*parts)


def solution(mesh):
    tokens = P(("seq", "head"), None)
    return jax.shard_map(
        per_device,
        mesh=mesh,
        in_specs=(tokens,) * 4 + (P("seq", None, None), P("seq", None)),
        out_specs=(tokens,) * 4,
        check_vma=False,
    )
```

```python
import functools
import math

import jax
import jax.numpy as jnp
from jax import lax
from jax.experimental import pallas as pl
from jax.experimental.pallas import tpu as pltpu
from jax.sharding import PartitionSpec as P

HD = 128
BF = jnp.bfloat16
F32 = jnp.float32
BIG = 3.0e38
NEG = -1.0e30


def split_seq(count):
    return {64: (4, 8, 2), 8: (2, 2, 2)}[count]


def dot_nn(a, b):
    return lax.dot_general(a, b, (((1,), (0,)), ((), ())), preferred_element_type=F32)


def dot_nt(a, b):
    return lax.dot_general(a, b, (((1,), (1,)), ((), ())), preferred_element_type=F32)


def dot_tn(a, b):
    return lax.dot_general(a, b, (((0,), (0,)), ((), ())), preferred_element_type=F32)


def spread(n):
    order = []
    for d in range(1, n // 2 + 1):
        order.append(d)
        if n - d != d:
            order.append(n - d)
    return order


def kernel(
    cfg,
    q_in, k_in, v_in, g_in, rows_in, extra_in,
    o_out, dq_out, dk_out, dv_out,
    kv, qg, skv, cap, sbuf, ebuf, stage, dloc, part, red1, red2, red3, psum,
    in_kv_send, in_qg_send, kv_recv, qg_recv,
    zg_send, zg_recv, xg_send, xg_recv, cg_send, cg_recv,
    cs_send, cs_recv, xs_send, xs_recv, zs_send, zs_recv,
    out_send, out_recv, rows_ref, extra_ref, small_sem, ring_ready, all_ready,
):
    nx, nz, nc, ny, heads, rows, summ, nblk = cfg
    group = rows * ny
    zrows = nz * summ
    tile = nc * zrows
    ins = (k_in, v_in, q_in, g_in)
    outs = (o_out, dq_out, dk_out, dv_out)
    factor = HD ** (-0.5)
    coef = factor * math.log2(math.e)

    seq = lax.axis_index("seq")
    y = lax.axis_index("head")
    x = seq // (nz * nc)
    z = (seq // nc) % nz
    c = seq % nc

    def at_y(yp):
        return (seq, yp)

    def at_z(zp):
        return (x * (nz * nc) + zp * nc + c, y)

    def at_x(xp):
        return (xp * (nz * nc) + z * nc + c, y)

    other = (x * (nz * nc) + z * nc + (1 - c), y)

    def remote(src, dst, send, recv, dev):
        return pltpu.make_async_remote_copy(
            src_ref=src, dst_ref=dst, send_sem=send, recv_sem=recv,
            device_id=dev, device_id_type=pl.DeviceIdType.MESH,
        )

    def signal(sem, dev):
        pl.semaphore_signal(sem, inc=1, device_id=dev, device_id_type=pl.DeviceIdType.MESH)

    barrier = pltpu.get_barrier_semaphore()
    for d in range(1, ny):
        yp = lax.rem(y + d, ny)

        @pl.when(yp != 0)
        def _():
            signal(barrier, at_y(yp))

    small = (
        pltpu.make_async_copy(rows_in, rows_ref, small_sem.at[0]),
        pltpu.make_async_copy(extra_in, extra_ref, small_sem.at[1]),
    )
    for copy in small:
        copy.start()

    @pl.when(y != 0)
    def _():
        pl.semaphore_wait(barrier, ny - 1)
        signal(ring_ready, at_y(0))

    rings = [at_z(lax.rem(z + d, nz)) for d in range(1, nz)]
    rings += [at_x(lax.rem(x + d, nx)) for d in range(1, nx)]
    rings += [other]

    @pl.when(y == 0)
    def _():
        pl.semaphore_wait(ring_ready, ny - 1)
        for dev in rings:
            signal(barrier, dev)

    def cols(owner, h):
        return pl.ds(pl.multiple_of((owner * heads + h) * HD, HD), HD)

    def own_rows(owner):
        return pl.ds(pl.multiple_of(owner * rows, rows), rows)

    def send_inputs(h, buf, pair, send, recv):
        for a in range(2):
            pltpu.make_async_copy(
                ins[pair + a].at[:, cols(y, h)], buf.at[h, a, own_rows(y), :], recv.at[h]
            ).start()
        for d in spread(ny):
            yp = lax.rem(y + d, ny)
            for a in range(2):
                remote(
                    ins[pair + a].at[:, cols(yp, h)], buf.at[h, a, own_rows(y), :],
                    send, recv.at[h], at_y(yp),
                ).start()

    @pl.loop(0, heads)
    def _(h):
        send_inputs(h, kv, 0, in_kv_send, kv_recv)

    @pl.loop(0, heads)
    def _(h):
        send_inputs(h, qg, 2, in_qg_send, qg_recv)

    def drain(ref, sem):
        pltpu.make_async_copy(ref, ref, sem).wait()

    for copy in small:
        copy.wait()
    onehot = (
        lax.broadcasted_iota(jnp.int32, (group, summ), 0) == rows_ref[...]
    ).astype(F32).astype(BF)

    blen = group // nblk
    ids = lax.broadcasted_iota(jnp.int32, (nblk, group), 0)
    pos = lax.broadcasted_iota(jnp.int32, (nblk, group), 1)
    block_hot = (pos // blen == ids).astype(F32)
    chosen = (extra_ref[0] == 1).astype(F32)
    by_key = dot_nn(chosen, block_hot)
    reads = dot_tn(by_key, block_hot)
    key_pos = lax.broadcasted_iota(jnp.int32, (group, group), 0)
    query_pos = lax.broadcasted_iota(jnp.int32, (group, group), 1)
    lag = query_pos // blen - key_pos // blen
    allowed = (key_pos <= query_pos) & ((lag == 0) | (lag == 1) | ((lag > 0) & (reads > 0.5)))
    cap[...] = jnp.where(allowed, BIG, NEG)

    zslot = pl.ds(pl.multiple_of(z * summ, summ), summ)

    def gather_z(h):
        drain(kv.at[h], kv_recv.at[h])
        for a in range(2):
            skv[h, a, x, c, zslot, :] = dot_tn(onehot, kv[h, a]).astype(BF)
        for d in spread(nz):
            mine = skv.at[h, :, x, c, zslot, :]
            remote(mine, mine, zg_send, zg_recv.at[h], at_z(lax.rem(z + d, nz))).start()

    def gather_x(h):
        drain(skv.at[h, :, 0, 0, pl.ds(0, (nz - 1) * summ), :], zg_recv.at[h])
        for d in spread(nx):
            mine = skv.at[h, :, x, c]
            remote(mine, mine, xg_send, xg_recv.at[h], at_x(lax.rem(x + d, nx))).start()

    def gather_c(h):
        drain(skv.at[h, :, pl.ds(0, nx - 1), 0], xg_recv.at[h])
        mine = skv.at[h, :, :, c]
        remote(mine, mine, cg_send, cg_recv.at[h], other).start()

    @pl.when(y == 0)
    def _():
        pl.semaphore_wait(barrier, len(rings))
        for d in range(1, ny):
            signal(all_ready, at_y(d))

    @pl.when(y != 0)
    def _():
        pl.semaphore_wait(all_ready, 1)

    @pl.loop(0, heads)
    def _(t):
        gather_z(t)

        @pl.when(t >= 1)
        def _():
            gather_x(t - 1)

        @pl.when(t >= 2)
        def _():
            gather_c(t - 2)

    row_id = lax.broadcasted_iota(jnp.int32, (tile, 1), 0)
    row_order = ((row_id % zrows) // summ) * nc + row_id // zrows
    is_before = row_order < z * nc + c

    def send_outputs(h, arrays):
        for a in arrays:
            pltpu.make_async_copy(
                stage.at[h, a, own_rows(y), :], outs[a].at[:, cols(y, h)], out_recv.at[a]
            ).start()
        for d in spread(ny):
            yp = lax.rem(y + d, ny)
            for a in arrays:
                remote(
                    stage.at[h, a, own_rows(yp), :], outs[a].at[:, cols(y, h)],
                    out_send, out_recv.at[a], at_y(yp),
                ).start()

    def attend(h, tiles):
        q = qg[h, 0]
        spans = [(pl.ds(0, group), kv[h, 0], kv[h, 1])]
        for xp in range(tiles):
            spans.append((
                pl.ds(group + xp * tile, tile),
                skv[h, 0, xp].reshape(tile, HD),
                skv[h, 1, xp].reshape(tile, HD),
            ))
        peak = None
        for i, (place, keys, _) in enumerate(spans):
            scores = dot_nt(keys, q)
            if i == 0:
                scores = jnp.minimum(scores, cap[...])
            elif i == tiles:
                scores = jnp.minimum(scores, jnp.where(is_before, BIG, NEG))
            sbuf[place, :] = scores
            top = jnp.max(scores, axis=0, keepdims=True)
            peak = top if peak is None else jnp.maximum(peak, top)
        peak = peak * coef
        mass = jnp.zeros((1, group), F32)
        acc = jnp.zeros((HD, group), F32)
        for place, _, vals in spans:
            e = jnp.exp2(sbuf[place, :] * coef - peak)
            eb = e.astype(BF)
            ebuf[place, :] = eb
            mass += jnp.sum(e, axis=0, keepdims=True)
            acc += dot_tn(vals, eb)
        inv = 1.0 / mass
        attn = (acc * inv).astype(BF).astype(F32)
        stage[h, 0] = attn.T.astype(BF)
        grad_t = qg[h, 1].astype(F32).T
        dot_row = jnp.sum(grad_t * attn, axis=0, keepdims=True) * inv
        grad_ts = grad_t * inv
        grad_tb = grad_ts.astype(BF)
        grad_b = grad_ts.T.astype(BF)
        acc = jnp.zeros((HD, group), F32)
        for i, (place, keys, vals) in enumerate(spans):
            eb = ebuf[place, :]
            ds = (eb.astype(F32) * (dot_nn(vals, grad_tb) - dot_row)).astype(BF)
            acc += dot_tn(keys, ds)
            dk = dot_nn(ds, q) * factor
            dv = dot_nn(eb, grad_b)
            if i == 0:
                dloc[h, 0] = dk
                dloc[h, 1] = dv
            else:
                for cc in range(nc):
                    rows_c = slice(cc * zrows, (cc + 1) * zrows)
                    part[h, i - 1, cc, 0] = dk[rows_c].astype(BF)
                    part[h, i - 1, cc, 1] = dv[rows_c].astype(BF)
        stage[h, 1] = (acc * factor).T.astype(BF)
        for xp in range(tiles, nx):
            part[h, xp] = jnp.zeros(part.shape[2:], BF)

    def attend_send(h):
        drain(qg.at[h], qg_recv.at[h])
        drain(skv.at[h, :, :, 0], cg_recv.at[h])
        for tiles in range(1, nx + 1):

            @pl.when(x == tiles - 1)
            def _():
                attend(h, tiles)

        send_outputs(h, (0, 1))

        mine = part.at[h, :, 1 - c]
        remote(mine, red1.at[h], cs_send, cs_recv.at[h], other).start()

    def reduce_c(h):
        drain(red1.at[h], cs_recv.at[h])

        @pl.loop(0, nx)
        def _(xp):
            part[h, xp, c] = (part[h, xp, c].astype(F32) + red1[h, xp].astype(F32)).astype(BF)

        for d in spread(nx):
            xp = lax.rem(x + d, nx)
            remote(part.at[h, xp, c], red2.at[h, x], xs_send, xs_recv.at[h], at_x(xp)).start()

    def reduce_x(h):
        drain(red2.at[h, pl.ds(0, nx - 1)], xs_recv.at[h])
        total = part[h, x, c].astype(F32)
        for d in range(1, nx):
            total += red2[h, lax.rem(x + d, nx)].astype(F32)
        psum[h] = total.astype(BF)
        for d in spread(nz):
            zp = lax.rem(z + d, nz)
            there = pl.ds(pl.multiple_of(zp * summ, summ), summ)
            remote(
                psum.at[h, :, there, :], red3.at[h, z], zs_send, zs_recv.at[h], at_z(zp)
            ).start()

    def reduce_z(h):
        drain(red3.at[h, pl.ds(0, nz - 1)], zs_recv.at[h])
        total = psum[h, :, zslot, :].astype(F32)
        for d in range(1, nz):
            total += red3[h, lax.rem(z + d, nz)].astype(F32)
        for a in range(2):
            high = total[a].astype(BF)
            low = (total[a] - high.astype(F32)).astype(BF)
            full = dloc[h, a] + dot_nn(onehot, high) + dot_nn(onehot, low)
            stage[h, 2 + a] = full.astype(BF)
        send_outputs(h, (2, 3))

    @pl.loop(0, heads + 3)
    def _(t):
        @pl.when(t < heads)
        def _():
            attend_send(t)

        @pl.when(t == 0)
        def _():
            gather_x(heads - 1)
            gather_c(heads - 2)

        @pl.when(t == 1)
        def _():
            gather_c(heads - 1)

        @pl.when((t >= 1) & (t < heads + 1))
        def _():
            reduce_c(t - 1)

        @pl.when((t >= 2) & (t < heads + 2))
        def _():
            reduce_x(t - 2)

        @pl.when(t >= 3)
        def _():
            reduce_z(t - 3)

    for a in range(4):
        drain(outs[a], out_recv.at[a])
    sent = pl.ds(0, (ny - 1) * rows)
    drain(kv.at[:, :, sent, :], in_kv_send)
    drain(qg.at[:, :, sent, :], in_qg_send)
    drain(stage.at[:, :, sent, :], out_send)
    drain(skv.at[:, :, 0, 0, pl.ds(0, (nz - 1) * summ), :], zg_send)
    drain(skv.at[:, :, pl.ds(0, nx - 1), 0], xg_send)
    drain(skv.at[:, :, :, 0], cg_send)
    drain(red1, cs_send)
    drain(red2.at[:, pl.ds(0, nx - 1)], xs_send)
    drain(red3.at[:, pl.ds(0, nz - 1)], zs_send)


def hand_over(a_in, b_in, c_in, d_in, a_out, b_out, c_out, d_out, sems):
    pieces = sems.shape[1]
    width = a_in.shape[1] // pieces
    pairs = ((a_in, a_out), (b_in, b_out), (c_in, c_out), (d_in, d_out))
    saves = []
    for j in range(pieces):
        for i, (src, dst) in enumerate(pairs):
            part = pl.ds(j * width, width)
            saves.append(pltpu.make_async_copy(src.at[:, part], dst.at[:, part], sems.at[i, j]))
    for save in saves:
        save.start()
    for save in saves:
        save.wait()


def per_device(queries, key_vectors, value_vectors, out_grads, extra_blocks, summary_rows):
    rows, feat = queries.shape
    ny = lax.axis_size("head")
    nx, nz, nc = split_seq(lax.axis_size("seq"))
    heads = feat // HD // ny
    summ = summary_rows.shape[1]
    nblk = extra_blocks.shape[1]
    group = rows * ny
    zrows = nz * summ
    keys = group + nx * nc * zrows
    cfg = (nx, nz, nc, ny, heads, rows, summ, nblk)
    dma = pltpu.SemaphoreType.DMA
    hbm = pl.BlockSpec(memory_space=pl.ANY)
    parts = pl.pallas_call(
        functools.partial(kernel, cfg),
        out_shape=[jax.ShapeDtypeStruct((rows, feat), BF)] * 4,
        in_specs=[hbm] * 6,
        out_specs=[hbm] * 4,
        scratch_shapes=[
            pltpu.VMEM((heads, 2, group, HD), BF),
            pltpu.VMEM((heads, 2, group, HD), BF),
            pltpu.VMEM((heads, 2, nx, nc, zrows, HD), BF),
            pltpu.VMEM((group, group), F32),
            pltpu.VMEM((keys, group), F32),
            pltpu.VMEM((keys, group), BF),
            pltpu.VMEM((heads, 4, group, HD), BF),
            pltpu.VMEM((heads, 2, group, HD), F32),
            pltpu.VMEM((heads, nx, nc, 2, zrows, HD), BF),
            pltpu.VMEM((heads, nx, 2, zrows, HD), BF),
            pltpu.VMEM((heads, nx, 2, zrows, HD), BF),
            pltpu.VMEM((heads, nz, 2, summ, HD), BF),
            pltpu.VMEM((heads, 2, zrows, HD), BF),
            dma(()), dma(()), dma((heads,)), dma((heads,)),
            dma(()), dma((heads,)), dma(()), dma((heads,)), dma(()), dma((heads,)),
            dma(()), dma((heads,)), dma(()), dma((heads,)), dma(()), dma((heads,)),
            dma(()), dma((4,)),
            pltpu.VMEM((1, summ), jnp.int32), pltpu.VMEM((1, nblk, nblk), jnp.int32), dma((2,)),
            pltpu.SemaphoreType.REGULAR, pltpu.SemaphoreType.REGULAR,
        ],
        compiler_params=pltpu.CompilerParams(
            collective_id=0, has_side_effects=True, vmem_limit_bytes=28 * 1024 * 1024
        ),
    )(
        *(
            pltpu.with_memory_space_constraint(arg, pltpu.HBM)
            for arg in (
                queries, key_vectors, value_vectors, out_grads, summary_rows, extra_blocks
            )
        ),
    )
    return pl.pallas_call(
        hand_over,
        out_shape=[jax.ShapeDtypeStruct((rows, feat), BF)] * 4,
        in_specs=[hbm] * 4,
        out_specs=[hbm] * 4,
        scratch_shapes=[dma((4, 2))],
        compiler_params=pltpu.CompilerParams(vmem_limit_bytes=4 * 1024 * 1024),
    )(*parts)


def solution(mesh):
    tokens = P(("seq", "head"), None)
    return jax.shard_map(
        per_device,
        mesh=mesh,
        in_specs=(tokens,) * 4 + (P("seq", None, None), P("seq", None)),
        out_specs=(tokens,) * 4,
        check_vma=False,
    )
```

```python
import functools
import math

import jax
import jax.numpy as jnp
from jax import lax
from jax.experimental import pallas as pl
from jax.experimental.pallas import tpu as pltpu
from jax.sharding import PartitionSpec as P

HD = 128
BF = jnp.bfloat16
F32 = jnp.float32
BIG = 3.0e38
NEG = -1.0e30


def split_seq(count):
    return {64: (4, 8, 2), 8: (2, 2, 2)}[count]


def dot_nn(a, b):
    return lax.dot_general(a, b, (((1,), (0,)), ((), ())), preferred_element_type=F32)


def dot_nt(a, b):
    return lax.dot_general(a, b, (((1,), (1,)), ((), ())), preferred_element_type=F32)


def dot_tn(a, b):
    return lax.dot_general(a, b, (((0,), (0,)), ((), ())), preferred_element_type=F32)


def spread(n):
    order = []
    for d in range(1, n // 2 + 1):
        order.append(d)
        if n - d != d:
            order.append(n - d)
    return order


def kernel(
    cfg,
    q_in, k_in, v_in, g_in, rows_in, extra_in,
    o_out, dq_out, dk_out, dv_out,
    kv, qg, skv, cap, sbuf, ebuf, stage, dloc, part, red1, red2, red3, psum,
    in_kv_send, in_qg_send, kv_recv, qg_recv,
    zg_send, zg_recv, xg_send, xg_recv, cg_send, cg_recv,
    cs_send, cs_recv, xs_send, xs_recv, zs_send, zs_recv,
    out_send, out_recv, rows_ref, extra_ref, small_sem, ring_ready, all_ready,
):
    nx, nz, nc, ny, heads, rows, summ, nblk = cfg
    group = rows * ny
    zrows = nz * summ
    tile = nc * zrows
    ins = (k_in, v_in, q_in, g_in)
    outs = (o_out, dq_out, dk_out, dv_out)
    factor = HD ** (-0.5)
    coef = factor * math.log2(math.e)

    seq = lax.axis_index("seq")
    y = lax.axis_index("head")
    x = seq // (nz * nc)
    z = (seq // nc) % nz
    c = seq % nc

    def at_y(yp):
        return (seq, yp)

    def at_z(zp):
        return (x * (nz * nc) + zp * nc + c, y)

    def at_x(xp):
        return (xp * (nz * nc) + z * nc + c, y)

    other = (x * (nz * nc) + z * nc + (1 - c), y)

    def remote(src, dst, send, recv, dev):
        return pltpu.make_async_remote_copy(
            src_ref=src, dst_ref=dst, send_sem=send, recv_sem=recv,
            device_id=dev, device_id_type=pl.DeviceIdType.MESH,
        )

    def signal(sem, dev):
        pl.semaphore_signal(sem, inc=1, device_id=dev, device_id_type=pl.DeviceIdType.MESH)

    barrier = pltpu.get_barrier_semaphore()
    for d in range(1, ny):
        yp = lax.rem(y + d, ny)

        @pl.when(yp != 0)
        def _():
            signal(barrier, at_y(yp))

    small = (
        pltpu.make_async_copy(rows_in, rows_ref, small_sem.at[0]),
        pltpu.make_async_copy(extra_in, extra_ref, small_sem.at[1]),
    )
    for copy in small:
        copy.start()

    @pl.when(y != 0)
    def _():
        pl.semaphore_wait(barrier, ny - 1)
        signal(ring_ready, at_y(0))

    rings = [at_z(lax.rem(z + d, nz)) for d in range(1, nz)]
    rings += [at_x(lax.rem(x + d, nx)) for d in range(1, nx)]
    rings += [other]

    @pl.when(y == 0)
    def _():
        pl.semaphore_wait(ring_ready, ny - 1)
        for dev in rings:
            signal(barrier, dev)

    def cols(owner, h):
        return pl.ds(pl.multiple_of((owner * heads + h) * HD, HD), HD)

    def own_rows(owner):
        return pl.ds(pl.multiple_of(owner * rows, rows), rows)

    def send_inputs(h, buf, pair, send, recv):
        for a in range(2):
            pltpu.make_async_copy(
                ins[pair + a].at[:, cols(y, h)], buf.at[h, a, own_rows(y), :], recv.at[h]
            ).start()
        for d in spread(ny):
            yp = lax.rem(y + d, ny)
            for a in range(2):
                remote(
                    ins[pair + a].at[:, cols(yp, h)], buf.at[h, a, own_rows(y), :],
                    send, recv.at[h], at_y(yp),
                ).start()

    @pl.loop(0, heads)
    def _(h):
        send_inputs(h, kv, 0, in_kv_send, kv_recv)

    @pl.loop(0, heads)
    def _(h):
        send_inputs(h, qg, 2, in_qg_send, qg_recv)

    def drain(ref, sem):
        pltpu.make_async_copy(ref, ref, sem).wait()

    for copy in small:
        copy.wait()
    onehot = (
        lax.broadcasted_iota(jnp.int32, (group, summ), 0) == rows_ref[...]
    ).astype(F32).astype(BF)

    blen = group // nblk
    ids = lax.broadcasted_iota(jnp.int32, (nblk, group), 0)
    pos = lax.broadcasted_iota(jnp.int32, (nblk, group), 1)
    block_hot = (pos // blen == ids).astype(F32)
    chosen = (extra_ref[0] == 1).astype(F32)
    by_key = dot_nn(chosen, block_hot)
    reads = dot_tn(by_key, block_hot)
    key_pos = lax.broadcasted_iota(jnp.int32, (group, group), 0)
    query_pos = lax.broadcasted_iota(jnp.int32, (group, group), 1)
    lag = query_pos // blen - key_pos // blen
    allowed = (key_pos <= query_pos) & ((lag == 0) | (lag == 1) | ((lag > 0) & (reads > 0.5)))
    cap[...] = jnp.where(allowed, BIG, NEG)

    zslot = pl.ds(pl.multiple_of(z * summ, summ), summ)

    def gather_z(h):
        drain(kv.at[h], kv_recv.at[h])
        for a in range(2):
            skv[h, a, x, c, zslot, :] = dot_tn(onehot, kv[h, a]).astype(BF)
        for d in spread(nz):
            mine = skv.at[h, :, x, c, zslot, :]
            remote(mine, mine, zg_send, zg_recv.at[h], at_z(lax.rem(z + d, nz))).start()

    def gather_x(h):
        drain(skv.at[h, :, 0, 0, pl.ds(0, (nz - 1) * summ), :], zg_recv.at[h])
        for d in spread(nx):
            mine = skv.at[h, :, x, c]
            remote(mine, mine, xg_send, xg_recv.at[h], at_x(lax.rem(x + d, nx))).start()

    def gather_c(h):
        drain(skv.at[h, :, pl.ds(0, nx - 1), 0], xg_recv.at[h])
        mine = skv.at[h, :, :, c]
        remote(mine, mine, cg_send, cg_recv.at[h], other).start()

    @pl.when(y == 0)
    def _():
        pl.semaphore_wait(barrier, len(rings))
        for d in range(1, ny):
            signal(all_ready, at_y(d))

    @pl.when(y != 0)
    def _():
        pl.semaphore_wait(all_ready, 1)

    @pl.loop(0, heads)
    def _(t):
        gather_z(t)

        @pl.when(t >= 1)
        def _():
            gather_x(t - 1)

        @pl.when(t >= 2)
        def _():
            gather_c(t - 2)

    row_id = lax.broadcasted_iota(jnp.int32, (tile, 1), 0)
    row_order = ((row_id % zrows) // summ) * nc + row_id // zrows
    is_before = row_order < z * nc + c

    def send_outputs(h, arrays):
        for a in arrays:
            pltpu.make_async_copy(
                stage.at[h, a, own_rows(y), :], outs[a].at[:, cols(y, h)], out_recv.at[a]
            ).start()
        for d in spread(ny):
            yp = lax.rem(y + d, ny)
            for a in arrays:
                remote(
                    stage.at[h, a, own_rows(yp), :], outs[a].at[:, cols(y, h)],
                    out_send, out_recv.at[a], at_y(yp),
                ).start()

    def attend(h, tiles):
        q = qg[h, 0]
        spans = [(pl.ds(0, group), kv[h, 0], kv[h, 1])]
        for xp in range(tiles):
            spans.append((
                pl.ds(group + xp * tile, tile),
                skv[h, 0, xp].reshape(tile, HD),
                skv[h, 1, xp].reshape(tile, HD),
            ))
        peak = None
        for i, (place, keys, _) in enumerate(spans):
            scores = dot_nt(keys, q)
            if i == 0:
                scores = jnp.minimum(scores, cap[...])
            elif i == tiles:
                scores = jnp.minimum(scores, jnp.where(is_before, BIG, NEG))
            sbuf[place, :] = scores
            top = jnp.max(scores, axis=0, keepdims=True)
            peak = top if peak is None else jnp.maximum(peak, top)
        peak = peak * coef
        mass = jnp.zeros((1, group), F32)
        acc = jnp.zeros((HD, group), F32)
        for place, _, vals in spans:
            e = jnp.exp2(sbuf[place, :] * coef - peak)
            eb = e.astype(BF)
            ebuf[place, :] = eb
            mass += jnp.sum(e, axis=0, keepdims=True)
            acc += dot_tn(vals, eb)
        inv = 1.0 / mass
        attn = (acc * inv).astype(BF).astype(F32)
        stage[h, 0] = attn.T.astype(BF)
        grad_t = qg[h, 1].astype(F32).T
        grad_ts = grad_t * inv
        grad_tb = grad_ts.astype(BF)
        grad_b = grad_ts.T.astype(BF)
        dot_row = jnp.sum(grad_tb.astype(F32) * attn, axis=0, keepdims=True)
        acc = jnp.zeros((HD, group), F32)
        for i, (place, keys, vals) in enumerate(spans):
            eb = ebuf[place, :]
            ds = (eb.astype(F32) * (dot_nn(vals, grad_tb) - dot_row)).astype(BF)
            acc += dot_tn(keys, ds)
            dk = dot_nn(ds, q) * factor
            dv = dot_nn(eb, grad_b)
            if i == 0:
                dloc[h, 0] = dk
                dloc[h, 1] = dv
            else:
                for cc in range(nc):
                    rows_c = slice(cc * zrows, (cc + 1) * zrows)
                    part[h, i - 1, cc, 0] = dk[rows_c].astype(BF)
                    part[h, i - 1, cc, 1] = dv[rows_c].astype(BF)
        stage[h, 1] = (acc * factor).T.astype(BF)
        for xp in range(tiles, nx):
            part[h, xp] = jnp.zeros(part.shape[2:], BF)

    def attend_send(h):
        drain(qg.at[h], qg_recv.at[h])
        drain(skv.at[h, :, :, 0], cg_recv.at[h])
        for tiles in range(1, nx + 1):

            @pl.when(x == tiles - 1)
            def _():
                attend(h, tiles)

        send_outputs(h, (0, 1))

        mine = part.at[h, :, 1 - c]
        remote(mine, red1.at[h], cs_send, cs_recv.at[h], other).start()

    def reduce_c(h):
        drain(red1.at[h], cs_recv.at[h])

        @pl.loop(0, nx)
        def _(xp):
            part[h, xp, c] = (part[h, xp, c].astype(F32) + red1[h, xp].astype(F32)).astype(BF)

        for d in spread(nx):
            xp = lax.rem(x + d, nx)
            remote(part.at[h, xp, c], red2.at[h, x], xs_send, xs_recv.at[h], at_x(xp)).start()

    def reduce_x(h):
        drain(red2.at[h, pl.ds(0, nx - 1)], xs_recv.at[h])
        total = part[h, x, c].astype(F32)
        for d in range(1, nx):
            total += red2[h, lax.rem(x + d, nx)].astype(F32)
        psum[h] = total.astype(BF)
        for d in spread(nz):
            zp = lax.rem(z + d, nz)
            there = pl.ds(pl.multiple_of(zp * summ, summ), summ)
            remote(
                psum.at[h, :, there, :], red3.at[h, z], zs_send, zs_recv.at[h], at_z(zp)
            ).start()

    def reduce_z(h):
        drain(red3.at[h, pl.ds(0, nz - 1)], zs_recv.at[h])
        total = psum[h, :, zslot, :].astype(F32)
        for d in range(1, nz):
            total += red3[h, lax.rem(z + d, nz)].astype(F32)
        for a in range(2):
            high = total[a].astype(BF)
            low = (total[a] - high.astype(F32)).astype(BF)
            full = dloc[h, a] + dot_nn(onehot, high) + dot_nn(onehot, low)
            stage[h, 2 + a] = full.astype(BF)
        send_outputs(h, (2, 3))

    @pl.loop(0, heads + 3)
    def _(t):
        @pl.when(t < heads)
        def _():
            attend_send(t)

        @pl.when(t == 0)
        def _():
            gather_x(heads - 1)
            gather_c(heads - 2)

        @pl.when(t == 1)
        def _():
            gather_c(heads - 1)

        @pl.when((t >= 1) & (t < heads + 1))
        def _():
            reduce_c(t - 1)

        @pl.when((t >= 2) & (t < heads + 2))
        def _():
            reduce_x(t - 2)

        @pl.when(t >= 3)
        def _():
            reduce_z(t - 3)

    for a in range(4):
        drain(outs[a], out_recv.at[a])
    sent = pl.ds(0, (ny - 1) * rows)
    drain(kv.at[:, :, sent, :], in_kv_send)
    drain(qg.at[:, :, sent, :], in_qg_send)
    drain(stage.at[:, :, sent, :], out_send)
    drain(skv.at[:, :, 0, 0, pl.ds(0, (nz - 1) * summ), :], zg_send)
    drain(skv.at[:, :, pl.ds(0, nx - 1), 0], xg_send)
    drain(skv.at[:, :, :, 0], cg_send)
    drain(red1, cs_send)
    drain(red2.at[:, pl.ds(0, nx - 1)], xs_send)
    drain(red3.at[:, pl.ds(0, nz - 1)], zs_send)


def hand_over(a_in, b_in, c_in, d_in, a_out, b_out, c_out, d_out, sems):
    pieces = sems.shape[1]
    width = a_in.shape[1] // pieces
    pairs = ((a_in, a_out), (b_in, b_out), (c_in, c_out), (d_in, d_out))
    saves = []
    for j in range(pieces):
        for i, (src, dst) in enumerate(pairs):
            part = pl.ds(j * width, width)
            saves.append(pltpu.make_async_copy(src.at[:, part], dst.at[:, part], sems.at[i, j]))
    for save in saves:
        save.start()
    for save in saves:
        save.wait()


def per_device(queries, key_vectors, value_vectors, out_grads, extra_blocks, summary_rows):
    rows, feat = queries.shape
    ny = lax.axis_size("head")
    nx, nz, nc = split_seq(lax.axis_size("seq"))
    heads = feat // HD // ny
    summ = summary_rows.shape[1]
    nblk = extra_blocks.shape[1]
    group = rows * ny
    zrows = nz * summ
    keys = group + nx * nc * zrows
    cfg = (nx, nz, nc, ny, heads, rows, summ, nblk)
    dma = pltpu.SemaphoreType.DMA
    hbm = pl.BlockSpec(memory_space=pl.ANY)
    parts = pl.pallas_call(
        functools.partial(kernel, cfg),
        out_shape=[jax.ShapeDtypeStruct((rows, feat), BF)] * 4,
        in_specs=[hbm] * 6,
        out_specs=[hbm] * 4,
        scratch_shapes=[
            pltpu.VMEM((heads, 2, group, HD), BF),
            pltpu.VMEM((heads, 2, group, HD), BF),
            pltpu.VMEM((heads, 2, nx, nc, zrows, HD), BF),
            pltpu.VMEM((group, group), F32),
            pltpu.VMEM((keys, group), F32),
            pltpu.VMEM((keys, group), BF),
            pltpu.VMEM((heads, 4, group, HD), BF),
            pltpu.VMEM((heads, 2, group, HD), F32),
            pltpu.VMEM((heads, nx, nc, 2, zrows, HD), BF),
            pltpu.VMEM((heads, nx, 2, zrows, HD), BF),
            pltpu.VMEM((heads, nx, 2, zrows, HD), BF),
            pltpu.VMEM((heads, nz, 2, summ, HD), BF),
            pltpu.VMEM((heads, 2, zrows, HD), BF),
            dma(()), dma(()), dma((heads,)), dma((heads,)),
            dma(()), dma((heads,)), dma(()), dma((heads,)), dma(()), dma((heads,)),
            dma(()), dma((heads,)), dma(()), dma((heads,)), dma(()), dma((heads,)),
            dma(()), dma((4,)),
            pltpu.VMEM((1, summ), jnp.int32), pltpu.VMEM((1, nblk, nblk), jnp.int32), dma((2,)),
            pltpu.SemaphoreType.REGULAR, pltpu.SemaphoreType.REGULAR,
        ],
        compiler_params=pltpu.CompilerParams(
            collective_id=0, has_side_effects=True, vmem_limit_bytes=28 * 1024 * 1024
        ),
    )(
        *(
            pltpu.with_memory_space_constraint(arg, pltpu.HBM)
            for arg in (
                queries, key_vectors, value_vectors, out_grads, summary_rows, extra_blocks
            )
        ),
    )
    return pl.pallas_call(
        hand_over,
        out_shape=[jax.ShapeDtypeStruct((rows, feat), BF)] * 4,
        in_specs=[hbm] * 4,
        out_specs=[hbm] * 4,
        scratch_shapes=[dma((4, 2))],
        compiler_params=pltpu.CompilerParams(vmem_limit_bytes=4 * 1024 * 1024),
    )(*parts)


def solution(mesh):
    tokens = P(("seq", "head"), None)
    return jax.shard_map(
        per_device,
        mesh=mesh,
        in_specs=(tokens,) * 4 + (P("seq", None, None), P("seq", None)),
        out_specs=(tokens,) * 4,
        check_vma=False,
    )
```
